32 devices in a mesh: row: 4 (over y, x), col: 8 (over z, core).
Axes of the slice: x: 2, y: 2, z: 4, core: 2. Of those that a mesh axis runs over, the one named last changes fastest.
Arguments:
- student_hidden: bfloat16 [4096, 1920], P(('row', 'col')), may hold values from -6 to 6
- projection: bfloat16 [1920, 768], replicated, may hold values from -0.125 to 0.125
- teacher: bfloat16 [2560, 768], P(('row', 'col')), may hold values from -6 to 6
- block_map: int32 [32, 3, 1024], P(('row', 'col')), may hold values from 0 to 127, as said below
- block_counts: int32 [32, 32], P(('row', 'col')), may hold values from 16 to 32, as said below
- interp_weights: float32 [64], replicated, may hold values from 0.1 to 1
Outputs:
- grad_hidden: bfloat16 [4096, 1920], P(('row', 'col'))
The draws below stay inside these ranges and needn't reach their ends.
Inputs may be any that keep to these rules, and one draw needn't show every extreme that they name: `block_map`: field 0 is a tubelet of the sending device below 80, field 1 a cell of the receiving device below 128, field 2 a level below 64. Slots to the sending device itself name cells near the tubelet's proportional position; slots to other devices name any of their cells. Dead slots hold values in range. `block_counts`: entry [s, d] counts the live slots from device s to device d, at the start of d's 32 slots; it is at least 16. In every draw some device receives 32 blocks from every device.
All inputs are finite; a program needn't handle non-finite values.
Results may differ from the reference program's by a relative error of at most 0.025.
Values may be sent and summed in bfloat16 or wider, within the bound.
No kernel may reach another device: no remote copies, remote signals or barrier semaphores. Data moves between devices by JAX's collectives and lax.ppermute only.
A program may use at most 64 MiB of HBM per device.

```python
import jax
import jax.numpy as jnp
from jax import lax

D_HID = 1920
D_REP = 768
TOK_DEV = 128
TUB_DEV = 80
CAP = 32
LEVELS = 64
TOKENS = 4096
TUBES = 2560
N_ROW = 4
DEVICES = 32


def draw_block_map(key, part):
    first, second, third, fifth = jax.random.split(jax.random.fold_in(key, 11), 4)
    shape = (DEVICES, DEVICES * CAP)
    sender = jnp.arange(DEVICES, dtype=jnp.int32)[:, None]
    receiver = (jnp.arange(DEVICES * CAP, dtype=jnp.int32) // CAP)[None, :]
    offset = receiver - sender
    tubes = jax.random.randint(first, shape, 0, TUB_DEV)
    jitter = max(TOK_DEV // 8, 1)
    centre = tubes * TOK_DEV // TUB_DEV + jax.random.randint(second, shape, -jitter, jitter + 1)
    centre = jnp.clip(centre, 0, TOK_DEV - 1)
    spread = jax.random.randint(third, shape, 0, TOK_DEV)
    cells = jnp.where(offset == 0, centre, spread)
    levels = jax.random.randint(fifth, shape, 0, LEVELS)
    return jnp.stack([tubes, cells, levels], axis=1).astype(jnp.int32)


def draw_block_counts(key, part):
    first, second = jax.random.split(jax.random.fold_in(key, 23))
    base = jax.random.randint(first, (DEVICES, DEVICES), CAP // 2, CAP + 1)
    busiest = jax.random.randint(second, (), 0, DEVICES)
    column = jnp.arange(DEVICES, dtype=jnp.int32)[None, :]
    counts = jnp.where(column == busiest, CAP, base)
    return counts.astype(jnp.int32)


def steps_of(own_key, dims, shards, least, top_value):
    level, own = 1.0, jax.random.fold_in(own_key, 6)
    for position, parts in shards:
        steps = jnp.exp(jax.random.uniform(jax.random.fold_in(own, position), (parts,), jnp.float32, least / len(shards), top_value / len(shards)))
        level = level * jnp.repeat(steps, dims[position] // parts).reshape([-1 if axis == position else 1 for axis in range(len(dims))])
    return level


def normal_values(stream_key, shape, scale, most, shards=(), kind=jnp.bfloat16):
    entries = scale * jax.random.normal(stream_key, shape, jnp.float32)
    if shards:
        entries = entries * steps_of(stream_key, shape, shards, -0.22, 0.18)
    return jnp.clip(entries, -most, most).astype(kind)


def setup_inputs(seed: int = 0) -> dict:
    streams_of = jax.random.split(jax.random.key(seed), 7)
    student_hidden = normal_values(streams_of[0], (TOKENS, D_HID), 1.0, 6.0, ((0, 32),))
    projection = normal_values(streams_of[1], (D_HID, D_REP), D_HID ** -0.5, 0.125)
    teacher = normal_values(streams_of[2], (TUBES, D_REP), 1.0, 6.0, ((0, 32),))
    block_map = draw_block_map(jax.random.fold_in(streams_of[6], 71), 0)
    block_counts = draw_block_counts(jax.random.fold_in(streams_of[6], 71), 0)
    interp_weights = jnp.clip(jax.random.uniform(streams_of[5], (LEVELS,), jnp.float32, 0.1, 1.0), 0.1, 1.0)
    return {"student_hidden": student_hidden, "projection": projection, "teacher": teacher, "block_map": block_map, "block_counts": block_counts, "interp_weights": interp_weights}


huber_delta = 0.05
norm_eps = 1e-06

def reference(student_hidden, projection, teacher, block_map, block_counts, interp_weights):
    devices = block_map.shape[0]
    slots = block_map.shape[2]
    per_peer = slots // devices
    tokens_dev = student_hidden.shape[0] // devices
    tubes_dev = teacher.shape[0] // devices
    width = teacher.shape[1]
    levels = interp_weights[block_map[:, 2, :]]
    live = (jnp.arange(per_peer, dtype=jnp.int32)[None, None, :] < block_counts[:, :, None]).reshape(devices, slots)
    scales = levels * live.astype(jnp.float32)
    tube_global = (block_map[:, 0, :] + (jnp.arange(devices, dtype=jnp.int32) * tubes_dev)[:, None]).astype(jnp.int32)
    cell_local = block_map[:, 1, :]

    def target_of(dest):
        start = (dest * per_peer).astype(jnp.int32)
        tubes = lax.dynamic_slice_in_dim(tube_global, start, per_peer, 1).reshape(-1)
        scale = lax.dynamic_slice_in_dim(scales, start, per_peer, 1).reshape(-1)
        cells = lax.dynamic_slice_in_dim(cell_local, start, per_peer, 1).reshape(-1)
        rows = teacher[tubes]
        contrib = (rows.astype(jnp.float32) * scale[:, None]).astype(jnp.bfloat16)
        onehot = (cells[None, :] == jnp.arange(tokens_dev, dtype=jnp.int32)[:, None]).astype(jnp.bfloat16)
        return jnp.dot(onehot, contrib, preferred_element_type=jnp.float32)
    target = lax.map(target_of, jnp.arange(devices, dtype=jnp.int32)).reshape(devices * tokens_dev, width)
    teacher_unit = (target * lax.rsqrt(lax.optimization_barrier(jnp.sum(target * target, axis=1, keepdims=True)) + norm_eps)).astype(jnp.bfloat16)
    proj = jnp.dot(student_hidden, projection, preferred_element_type=jnp.float32)
    inverse = lax.rsqrt(lax.optimization_barrier(jnp.sum(proj * proj, axis=1, keepdims=True)) + norm_eps)
    unit = proj * inverse
    student_unit = unit.astype(jnp.bfloat16)
    total = student_unit.shape[0]
    strip_rows = total // N_ROW
    contract = (((1,), (1,)), ((), ()))

    def strip(start):
        block_s = lax.dynamic_slice_in_dim(student_unit, start, strip_rows, 0)
        block_t = lax.dynamic_slice_in_dim(teacher_unit, start, strip_rows, 0)
        gram_s = lax.dot_general(block_s, student_unit, contract, preferred_element_type=jnp.float32)
        gram_t = lax.dot_general(block_t, teacher_unit, contract, preferred_element_type=jnp.float32)
        slope = jnp.clip((gram_s - gram_t) / huber_delta, -1.0, 1.0).astype(jnp.bfloat16)
        return 2.0 * jnp.dot(slope, student_unit, preferred_element_type=jnp.float32)
    starts = jnp.arange(N_ROW, dtype=jnp.int32) * strip_rows
    grad_unit = lax.map(strip, starts).reshape(total, width)
    along = lax.optimization_barrier(jnp.sum(unit * grad_unit, axis=1, keepdims=True))
    grad_proj = ((grad_unit - unit * along) * inverse).astype(jnp.bfloat16)
    grad_hidden = lax.dot_general(grad_proj, projection, contract, preferred_element_type=jnp.float32)
    return grad_hidden.astype(jnp.bfloat16)
```

```python
import functools

import jax
import jax.numpy as jnp
from jax import lax
from jax.experimental import pallas as pl
from jax.experimental.pallas import tpu as pltpu
from jax.sharding import PartitionSpec as P

huber_delta = 0.05
norm_eps = 1e-06
CORES = 2
LANES = 128
SPAN = 256
F32 = jnp.float32
BF16 = jnp.bfloat16
VMEM = pl.BlockSpec(memory_space=pltpu.VMEM)
SMEM = pl.BlockSpec(memory_space=pltpu.SMEM)
NT = (((1,), (1,)), ((), ()))


def round_up(value, unit):
    return -(-value // unit) * unit


def params(mib):
    return pltpu.CompilerParams(vmem_limit_bytes=mib * 1024 * 1024)


def pack_kernel(per_peer, counts_ref, table_ref, teacher_ref, map_ref, out_ref):
    tubes = teacher_ref.shape[0]
    slots = map_ref.shape[2]
    rows = slots // SPAN
    out_ref[0:tubes, :] = teacher_ref[...]
    fields = []
    for f in range(3):
        parts = [map_ref[0, f : f + 1, q * SPAN : (q + 1) * SPAN] for q in range(rows)]
        fields.append(jnp.concatenate(parts, axis=0))
    tube, cell, level = fields
    weight = lax.fori_loop(
        0,
        table_ref.shape[0],
        lambda i, w: jnp.where(level == i, table_ref[i], w),
        jnp.zeros((rows, SPAN), F32),
    )
    row = lax.broadcasted_iota(jnp.int32, (rows, SPAN), 0)
    lane = lax.broadcasted_iota(jnp.int32, (rows, SPAN), 1)
    receiver = row * (SPAN // per_peer) + lane // per_peer
    count = lax.fori_loop(
        0,
        counts_ref.shape[1],
        lambda i, c: jnp.where(receiver == i, counts_ref[0, i], c),
        jnp.zeros((rows, SPAN), jnp.int32),
    )
    weight = jnp.where(lane % per_peer < count, weight, 0.0)
    block = jnp.concatenate([tube.astype(F32), cell.astype(F32), weight], axis=1)
    pad = out_ref.shape[0] - tubes - rows
    if pad:
        block = jnp.concatenate([block, jnp.zeros((pad, block.shape[1]), F32)], axis=0)
    out_ref[tubes:, 0 : 3 * SPAN] = block.astype(BF16)


def pack(teacher, block_map, block_counts, interp_weights):
    tubes, width = teacher.shape
    slots = block_map.shape[2]
    peers = block_counts.shape[1]
    rows = tubes + round_up(slots // SPAN, 8)
    return pl.pallas_call(
        functools.partial(pack_kernel, slots // peers),
        out_shape=jax.ShapeDtypeStruct((rows, width), BF16),
        in_specs=[SMEM, SMEM, VMEM, VMEM],
        out_specs=VMEM,
        compiler_params=params(8),
    )(block_counts, interp_weights, teacher, block_map)


def student_kernel(hidden_ref, projection_ref, unit_ref, inverse_ref, student_ref):
    proj = jnp.dot(hidden_ref[...], projection_ref[...], preferred_element_type=F32)
    inverse = lax.rsqrt(jnp.sum(proj * proj, axis=1, keepdims=True) + norm_eps)
    unit = proj * inverse
    unit_ref[...] = unit
    inverse_ref[...] = jnp.broadcast_to(inverse, inverse_ref.shape)
    student_ref[...] = unit.astype(BF16)


def project(hidden, projection):
    tokens, width = hidden.shape[0], projection.shape[1]
    return pl.pallas_call(
        student_kernel,
        out_shape=(
            jax.ShapeDtypeStruct((tokens, width), F32),
            jax.ShapeDtypeStruct((tokens, LANES), F32),
            jax.ShapeDtypeStruct((tokens, width), BF16),
        ),
        in_specs=[VMEM, VMEM],
        out_specs=(VMEM, VMEM, VMEM),
        compiler_params=params(16),
    )(hidden, projection)


def target_kernel(tubes, per_peer, tokens, first, dests_ref, *refs):
    group = SPAN // per_peer
    payloads = refs[:group]
    if first:
        out_ref, teacher, table, matrix = refs[group:]
        total_ref = None
    else:
        total_ref, out_ref, teacher, table, matrix = refs[group:]
    count = dests_ref.shape[0]
    depth = group * tubes
    for s, payload in enumerate(payloads):
        teacher[s * tubes : (s + 1) * tubes, :] = payload[0:tubes, :]
        rows = payload[tubes:, 0 : 3 * SPAN].astype(F32)
        for q in range(table.shape[0]):
            table[q, s : s + 1, :] = rows[q : q + 1, :]
    sender = lax.broadcasted_iota(jnp.int32, (group, SPAN), 0)
    lane = lax.broadcasted_iota(jnp.int32, (group, SPAN), 1)
    window = lane < per_peer
    diagonal = lane // per_peer == sender
    offset = (lax.broadcasted_iota(jnp.int32, (1, SPAN), 1) // per_peer * tubes).astype(F32)
    cells = lax.broadcasted_iota(jnp.int32, (tokens, SPAN), 0).astype(F32)
    places = lax.broadcasted_iota(jnp.int32, (depth, SPAN), 0).astype(F32)

    def build(i, carry):
        dest = dests_ref[i]
        slots = table[dest // group]
        shift = (SPAN - (dest % group) * per_peer) % SPAN
        picked = []
        for f in range(3):
            part = pltpu.roll(slots[:, f * SPAN : (f + 1) * SPAN], shift, 1)
            part = jnp.where(window, part, 0.0)
            step = per_peer
            while step < SPAN:
                part = part + pltpu.roll(part, step, 1)
                step *= 2
            picked.append(jnp.sum(jnp.where(diagonal, part, 0.0), axis=0, keepdims=True))
        tube, cell, weight = picked
        left = jnp.where(cells == cell, 1.0, 0.0).astype(BF16)
        right = jnp.where(places == tube + offset, weight, 0.0).astype(BF16)
        block = lax.dot_general(left, right, NT, preferred_element_type=F32)
        matrix[pl.ds(pl.multiple_of(i * tokens, tokens), tokens), :] = block.astype(BF16)
        return carry

    lax.fori_loop(0, count, build, 0)
    part = jnp.dot(matrix[...], teacher[...], preferred_element_type=F32)
    out_ref[...] = part if first else total_ref[...] + part


def add_targets(total, payloads, dests, tubes, per_peer, tokens):
    rows, width = payloads[0].shape
    group = SPAN // per_peer
    count = dests.shape[0]
    first = total is None
    extra = () if first else (total,)
    return pl.pallas_call(
        functools.partial(target_kernel, tubes, per_peer, tokens, first),
        out_shape=jax.ShapeDtypeStruct((count * tokens, width), F32),
        in_specs=[SMEM] + [VMEM] * (group + len(extra)),
        out_specs=VMEM,
        scratch_shapes=[
            pltpu.VMEM((group * tubes, width), BF16),
            pltpu.VMEM((rows - tubes, group, 3 * SPAN), F32),
            pltpu.VMEM((count * tokens, group * tubes), BF16),
        ],
        input_output_aliases={} if first else {1 + group: 0},
        compiler_params=params(40),
    )(dests, *payloads, *extra)


def relation_kernel(n_row, n_col, targets_ref, *refs):
    blocks = n_row + n_col - 1
    students = refs[:blocks]
    own_ref = refs[blocks]
    others = refs[blocks + 1 : blocks + n_col]
    student, teacher = refs[blocks + n_col :]
    tokens = students[0].shape[0]
    for i, block in enumerate(students):
        student[i * tokens : (i + 1) * tokens, :] = block[...]
    total = targets_ref[...]
    teacher[...] = (
        total * lax.rsqrt(jnp.sum(total * total, axis=1, keepdims=True) + norm_eps)
    ).astype(BF16)
    rows_s = student[0 : n_row * tokens, :]
    rows_t = teacher[0 : n_row * tokens, :]
    for j in range(n_col):
        at = (n_row + j - 1) * tokens if j else 0
        gram_s = lax.dot_general(
            student[at : at + tokens, :], rows_s, NT, preferred_element_type=F32
        )
        gram_t = lax.dot_general(
            teacher[at : at + tokens, :], rows_t, NT, preferred_element_type=F32
        )
        slope = jnp.clip((gram_s - gram_t) / huber_delta, -1.0, 1.0).astype(BF16)
        grad = jnp.dot(slope, rows_s, preferred_element_type=F32)
        if j:
            others[j - 1][...] = grad.astype(BF16)
        else:
            own_ref[...] = grad


def relate(targets, row_students, column_students):
    tokens, width = row_students[0].shape
    n_row, n_col = len(row_students), len(column_students) + 1
    blocks = n_row + n_col - 1
    return pl.pallas_call(
        functools.partial(relation_kernel, n_row, n_col),
        out_shape=(jax.ShapeDtypeStruct((tokens, width), F32),)
        + (jax.ShapeDtypeStruct((tokens, width), BF16),) * (n_col - 1),
        in_specs=[VMEM] * (1 + blocks),
        out_specs=(VMEM,) * n_col,
        scratch_shapes=[
            pltpu.VMEM((blocks * tokens, width), BF16),
            pltpu.VMEM((blocks * tokens, width), BF16),
        ],
        compiler_params=params(40),
    )(targets, *row_students, *column_students)


def finish_kernel(unit_ref, inverse_ref, projection_ref, own_ref, *refs):
    grad = own_ref[...]
    for other in refs[:-1]:
        grad = grad + other[...].astype(F32)
    grad = 2.0 * grad
    unit = unit_ref[...]
    along = jnp.sum(unit * grad, axis=1, keepdims=True)
    grad_proj = ((grad - unit * along) * inverse_ref[:, 0:1]).astype(BF16)
    refs[-1][...] = lax.dot_general(
        grad_proj, projection_ref[...], NT, preferred_element_type=F32
    ).astype(BF16)


def finish(unit, inverse, projection, own, others):
    return pl.pallas_call(
        finish_kernel,
        out_shape=jax.ShapeDtypeStruct((unit.shape[0], projection.shape[0]), BF16),
        in_specs=[VMEM] * (4 + len(others)),
        out_specs=VMEM,
        compiler_params=params(16),
    )(unit, inverse, projection, own, *others)


def local(n_row, n_col, student_hidden, projection, teacher, block_map, block_counts, interp_weights):
    tubes = teacher.shape[0]
    tokens = student_hidden.shape[0]
    per_peer = block_map.shape[2] // block_counts.shape[1]
    n_z = n_col // CORES
    row, col = lax.axis_index("row"), lax.axis_index("col")

    def along_row(x, k):
        return lax.ppermute(x, "row", [(i, i ^ k) for i in range(n_row)])

    def along_col(x, k):
        return lax.ppermute(x, "col", [(i, i ^ k) for i in range(n_col)])

    dests = jnp.stack(
        [row * n_col + (col ^ k) for k in range(n_col)]
        + [(row ^ j) * n_col + col for j in range(1, n_row)]
    ).astype(jnp.int32)

    payload = pack(teacher, block_map, block_counts, interp_weights)
    planes = [payload] + [along_col(payload, CORES * k) for k in range(1, n_z)]
    unit, inverse, student = project(student_hidden, projection)
    total = None
    group = SPAN // per_peer
    for plane in planes:
        held = [plane] + [along_row(plane, j) for j in range(1, n_row)]
        held = held + [along_col(x, 1) for x in held]
        for at in range(0, len(held), group):
            total = add_targets(total, held[at : at + group], dests, tubes, per_peer, tokens)
    half = [student] + [along_col(student, CORES * k) for k in range(1, n_z)]
    rows = []
    for x in half:
        rows += [x, along_col(x, 1)]
    columns = [along_row(student, j) for j in range(1, n_row)]
    own, *others = relate(total, rows, columns)
    arrived = [along_row(x, j + 1) for j, x in enumerate(others)]
    return finish(unit, inverse, projection, own, arrived)


def solution(mesh):
    in_specs = (
        P(("row", "col"), None),
        P(),
        P(("row", "col"), None),
        P(("row", "col"), None, None),
        P(("row", "col"), None),
        P(),
    )
    out_specs = P(("row", "col"), None)
    body = functools.partial(local, mesh.shape["row"], mesh.shape["col"])
    return jax.shard_map(body, mesh=mesh, in_specs=in_specs, out_specs=out_specs, check_vma=False)
```

```python
import functools

import jax
import jax.numpy as jnp
from jax import lax
from jax.experimental import pallas as pl
from jax.experimental.pallas import tpu as pltpu
from jax.sharding import PartitionSpec as P

huber_delta = 0.05
norm_eps = 1e-06
CORES = 2
LANES = 128
F32 = jnp.float32
BF16 = jnp.bfloat16
VMEM = pl.BlockSpec(memory_space=pltpu.VMEM)
SMEM = pl.BlockSpec(memory_space=pltpu.SMEM)
HBM = pl.BlockSpec(memory_space=pltpu.HBM)
NT = (((1,), (1,)), ((), ()))


def round_up(value, unit):
    return -(-value // unit) * unit


def params(mib):
    return pltpu.CompilerParams(vmem_limit_bytes=mib * 1024 * 1024)


def prepare_kernel(
    per_peer,
    counts_hbm,
    table_hbm,
    map_hbm,
    teacher_hbm,
    hidden_hbm,
    projection_hbm,
    out_ref,
    unit_ref,
    inverse_ref,
    student_ref,
    counts,
    table,
    fields,
    teacher,
    hidden,
    projection,
    sems,
):
    copies = [
        pltpu.make_async_copy(source, target, sems.at[i])
        for i, (source, target) in enumerate(
            (
                (counts_hbm, counts),
                (table_hbm, table),
                (map_hbm, fields),
                (teacher_hbm, teacher),
                (hidden_hbm, hidden),
                (projection_hbm, projection),
            )
        )
    ]
    for copy in copies:
        copy.start()
    for copy in copies[:4]:
        copy.wait()
    tubes = teacher.shape[0]
    rows = fields.shape[0] // 3
    out_ref[0:tubes, :] = teacher[...]
    tube, cell, level = (fields[f * rows : (f + 1) * rows, :] for f in range(3))
    weight = jnp.zeros((rows, LANES), F32)
    for i in range(table.shape[0]):
        weight = jnp.where(level == i, table[i], weight)
    row = lax.broadcasted_iota(jnp.int32, (rows, LANES), 0)
    lane = lax.broadcasted_iota(jnp.int32, (rows, LANES), 1)
    receiver = row * (LANES // per_peer) + lane // per_peer
    count = jnp.zeros((rows, LANES), jnp.int32)
    for i in range(counts.shape[0]):
        count = jnp.where(receiver == i, counts[i], count)
    weight = jnp.where(lane % per_peer < count, weight, 0.0)
    block = jnp.concatenate([tube.astype(F32), cell.astype(F32), weight], axis=1)
    out_ref[tubes:, 0 : 3 * LANES] = block.astype(BF16)
    out_ref[tubes:, 3 * LANES :] = jnp.zeros((rows, out_ref.shape[1] - 3 * LANES), BF16)
    for copy in copies[4:]:
        copy.wait()
    proj = jnp.dot(hidden[...], projection[...], preferred_element_type=F32)
    inverse = lax.rsqrt(jnp.sum(proj * proj, axis=1, keepdims=True) + norm_eps)
    unit = proj * inverse
    unit_ref[...] = unit
    inverse_ref[...] = jnp.broadcast_to(inverse, inverse_ref.shape)
    student_ref[...] = unit.astype(BF16)


def prepare(hidden, projection, teacher, block_map, block_counts, interp_weights):
    tubes, width = teacher.shape
    tokens = hidden.shape[0]
    slots = block_map.shape[2]
    peers = block_counts.shape[1]
    rows = slots // LANES
    return pl.pallas_call(
        functools.partial(prepare_kernel, slots // peers),
        out_shape=(
            jax.ShapeDtypeStruct((tubes + rows, width), BF16),
            jax.ShapeDtypeStruct((tokens, width), F32),
            jax.ShapeDtypeStruct((tokens, LANES), F32),
            jax.ShapeDtypeStruct((tokens, width), BF16),
        ),
        in_specs=[HBM] * 6,
        out_specs=(VMEM,) * 4,
        scratch_shapes=[
            pltpu.SMEM((peers,), jnp.int32),
            pltpu.SMEM(interp_weights.shape, F32),
            pltpu.VMEM((3 * rows, LANES), jnp.int32),
            pltpu.VMEM(teacher.shape, BF16),
            pltpu.VMEM(hidden.shape, BF16),
            pltpu.VMEM(projection.shape, BF16),
            pltpu.SemaphoreType.DMA((6,)),
        ],
    )(
        block_counts.reshape(peers),
        interp_weights,
        block_map.reshape(3 * rows, LANES),
        teacher,
        hidden,
        projection,
    )


def pick(slots, window, per_peer, masks):
    shift = (LANES - window * per_peer) % LANES
    lane = lax.broadcasted_iota(jnp.int32, (slots.shape[0], LANES), 1)
    fields = []
    for f in range(3):
        part = pltpu.roll(slots[:, f * LANES : (f + 1) * LANES], shift, 1)
        part = jnp.where(lane < per_peer, part, 0.0)
        step = per_peer
        while step < LANES:
            part = part + pltpu.roll(part, step, 1)
            step *= 2
        fields.append(part)
    return [
        [jnp.sum(jnp.where(mask, part, 0.0), axis=0, keepdims=True) for part in fields]
        for mask in masks
    ]


def target_kernel(tubes, per_peer, tokens, n_held, first, n_last, dests_ref, *refs):
    held = refs[:n_held]
    outs = refs[n_held + (0 if first else 1) : -3]
    teacher, table, matrix = refs[-3:]
    group = LANES // per_peer
    depth = round_up(group * tubes, LANES)
    rows = tubes + table.shape[1]
    count = matrix.shape[0] // tokens
    groups = matrix.shape[1] // depth
    s = 0
    for h in held:
        for at in range(0, h.shape[0], rows):
            base = s // group * depth + s % group * tubes
            teacher[base : base + tubes, :] = h[at : at + tubes, :]
            slots = h[at + tubes : at + rows, 0 : 3 * LANES].astype(F32)
            for q in range(rows - tubes):
                table[s // 8, q, s % 8 : s % 8 + 1, :] = slots[q : q + 1, :]
            s += 1
    pad = depth - group * tubes
    if pad:
        for g in range(groups):
            teacher[(g + 1) * depth - pad : (g + 1) * depth, :] = jnp.zeros(
                (pad, teacher.shape[1]), BF16
            )
    sender = lax.broadcasted_iota(jnp.int32, (8, LANES), 0)
    lane = lax.broadcasted_iota(jnp.int32, (8, LANES), 1)
    masks = [sender == lane // per_peer + at for at in range(0, 8, group)]
    offset = (lax.broadcasted_iota(jnp.int32, (1, LANES), 1) // per_peer * tubes).astype(F32)
    cells = lax.broadcasted_iota(jnp.int32, (tokens, LANES), 0).astype(F32)
    places = lax.broadcasted_iota(jnp.int32, (depth, LANES), 0).astype(F32)
    for i in range(count):
        dest = dests_ref[i]
        picked = []
        for e in range(table.shape[0]):
            picked += pick(table[e, dest // group], dest % group, per_peer, masks)
        for g in range(groups):
            tube, cell, weight = picked[g]
            left = jnp.where(cells == cell, 1.0, 0.0).astype(BF16)
            right = jnp.where(places == tube + offset, weight, 0.0).astype(BF16)
            block = lax.dot_general(left, right, NT, preferred_element_type=F32)
            matrix[i * tokens : (i + 1) * tokens, g * depth : (g + 1) * depth] = block.astype(BF16)
    total = jnp.dot(matrix[...], teacher[...], preferred_element_type=F32)
    if not first:
        total = total + refs[n_held][...]
    if n_last is None:
        outs[0][...] = total
        return
    total = total * lax.rsqrt(jnp.sum(total * total, axis=1, keepdims=True) + norm_eps)
    outs[0][...] = total[0:n_last, :].astype(BF16)
    outs[1][...] = total[n_last:, :].astype(BF16)


def add_targets(total, held, dests, tubes, per_peer, tokens, rows, n_last):
    width = held[0].shape[1]
    group = LANES // per_peer
    senders = sum(h.shape[0] for h in held) // rows
    groups = senders // group
    depth = round_up(group * tubes, LANES)
    count = dests.shape[0]
    first = total is None
    extra = () if first else (total,)
    if n_last is None:
        out_shape = jax.ShapeDtypeStruct((count * tokens, width), F32)
        out_specs = VMEM
    else:
        out_shape = tuple(
            jax.ShapeDtypeStruct((n, width), BF16) for n in (n_last, count * tokens - n_last)
        )
        out_specs = (VMEM, VMEM)
    return pl.pallas_call(
        functools.partial(target_kernel, tubes, per_peer, tokens, len(held), first, n_last),
        out_shape=out_shape,
        in_specs=[SMEM] + [VMEM] * (len(held) + len(extra)),
        out_specs=out_specs,
        scratch_shapes=[
            pltpu.VMEM((groups * depth, width), BF16),
            pltpu.VMEM((-(-senders // 8), rows - tubes, 8, 3 * LANES), F32),
            pltpu.VMEM((count * tokens, groups * depth), BF16),
        ],
        input_output_aliases={} if first or n_last else {1 + len(held): 0},
        compiler_params=params(40),
    )(dests, *held, *extra)


def relation_kernel(n_rows, n_columns, last, *refs):
    students = refs[:n_rows]
    columns = refs[n_rows : n_rows + n_columns]
    teacher_ref, own_ref, column_ref = refs[n_rows + n_columns : n_rows + n_columns + 3]
    rest = refs[n_rows + n_columns + 3 : -3]
    student, column_s, column_t = refs[-3:]
    tokens = students[0].shape[0]
    for i, block in enumerate(students):
        student[i * tokens : (i + 1) * tokens, :] = block[...]
    at = 0
    for block in columns:
        column_s[at : at + block.shape[0], :] = block[...]
        at += block.shape[0]
    column_t[0:tokens, :] = own_ref[0:tokens, :]
    column_t[tokens:, :] = column_ref[...]
    gram_s = lax.dot_general(column_s[...], student[...], NT, preferred_element_type=F32)
    gram_t = lax.dot_general(column_t[...], teacher_ref[...], NT, preferred_element_type=F32)
    slope = jnp.clip((gram_s - gram_t) / huber_delta, -1.0, 1.0).astype(BF16)
    grad = jnp.dot(slope, student[...], preferred_element_type=F32)
    if not last:
        rest[0][...] = grad
        return
    grad = grad + rest[0][...]
    rest[1][...] = grad[0:tokens, :]
    for j, out in enumerate(rest[2:]):
        out[...] = grad[(j + 1) * tokens : (j + 2) * tokens, :].astype(BF16)


def relate(students, columns, teacher, own, column_teacher, partial):
    tokens, width = students[0].shape
    total = sum(c.shape[0] for c in columns)
    n_col = total // tokens
    last = partial is not None
    if last:
        out_shape = (jax.ShapeDtypeStruct((tokens, width), F32),) + (
            jax.ShapeDtypeStruct((tokens, width), BF16),
        ) * (n_col - 1)
        out_specs = (VMEM,) * n_col
        extra = (partial,)
    else:
        out_shape = jax.ShapeDtypeStruct((total, width), F32)
        out_specs = VMEM
        extra = ()
    return pl.pallas_call(
        functools.partial(relation_kernel, len(students), len(columns), last),
        out_shape=out_shape,
        in_specs=[VMEM] * (len(students) + len(columns) + 3 + len(extra)),
        out_specs=out_specs,
        scratch_shapes=[
            pltpu.VMEM((len(students) * tokens, width), BF16),
            pltpu.VMEM((total, width), BF16),
            pltpu.VMEM((total, width), BF16),
        ],
        compiler_params=params(40),
    )(*students, *columns, teacher, own, column_teacher, *extra)


def finish_kernel(unit_ref, inverse_ref, projection_ref, own_ref, *refs):
    grad = own_ref[...]
    for other in refs[:-1]:
        grad = grad + other[...].astype(F32)
    grad = 2.0 * grad
    unit = unit_ref[...]
    along = jnp.sum(unit * grad, axis=1, keepdims=True)
    grad_proj = ((grad - unit * along) * inverse_ref[:, 0:1]).astype(BF16)
    refs[-1][...] = lax.dot_general(
        grad_proj, projection_ref[...], NT, preferred_element_type=F32
    ).astype(BF16)


def finish(unit, inverse, projection, own, others):
    return pl.pallas_call(
        finish_kernel,
        out_shape=jax.ShapeDtypeStruct((unit.shape[0], projection.shape[0]), BF16),
        in_specs=[VMEM] * (4 + len(others)),
        out_specs=VMEM,
        compiler_params=params(16),
    )(unit, inverse, projection, own, *others)


def doubled(x, exchange, steps):
    held, offsets = [x], [0]
    for step in steps:
        if len(held) > 1:
            held = [jnp.concatenate(held, axis=0)]
        held.append(exchange(held[0], step))
        offsets += [o ^ step for o in offsets]
    return held, offsets


def local(n_row, n_col, student_hidden, projection, teacher, block_map, block_counts, interp_weights):
    tubes = teacher.shape[0]
    tokens = student_hidden.shape[0]
    per_peer = block_map.shape[2] // block_counts.shape[1]
    n_z = n_col // CORES
    row, col = lax.axis_index("row"), lax.axis_index("col")
    steps = [1 << b for b in range(n_row.bit_length() - 1)]

    def along_row(x, k):
        return lax.ppermute(x, "row", [(i, i ^ k) for i in range(n_row)])

    def along_col(x, k):
        return lax.ppermute(x, "col", [(i, i ^ k) for i in range(n_col)])

    payload, unit, inverse, student = prepare(
        student_hidden, projection, teacher, block_map, block_counts, interp_weights
    )
    planes = [payload] + [along_col(payload, CORES * k) for k in range(1, n_z)]
    columns, offsets = doubled(student, along_row, steps[::-1])
    dests = jnp.stack(
        [row * n_col + (col ^ (CORES * k)) for k in range(n_z)]
        + [(row ^ o) * n_col + col for o in offsets[1:]]
    ).astype(jnp.int32)
    total = None
    for k, plane in enumerate(planes):
        held, _ = doubled(plane, along_row, steps[::-1] if k == n_z - 1 else steps)
        held = held + [along_col(x, 1) for x in held]
        n_last = n_z * tokens if k == n_z - 1 else None
        total = add_targets(total, held, dests, tubes, per_peer, tokens, payload.shape[0], n_last)
    own, column = total
    partner = along_col(own, 1)
    rows = [student] + [along_col(student, CORES * k) for k in range(1, n_z)]
    partner_rows = [along_col(x, 1) for x in rows]
    grad = relate(rows, columns, own, own, column, None)
    mine, *others = relate(partner_rows, columns, partner, own, column, grad)
    arrived = [along_row(x, o) for x, o in zip(others, offsets[1:])]
    return finish(unit, inverse, projection, mine, arrived)


def solution(mesh):
    in_specs = (
        P(("row", "col"), None),
        P(),
        P(("row", "col"), None),
        P(("row", "col"), None, None),
        P(("row", "col"), None),
        P(),
    )
    out_specs = P(("row", "col"), None)
    body = functools.partial(local, mesh.shape["row"], mesh.shape["col"])
    return jax.shard_map(body, mesh=mesh, in_specs=in_specs, out_specs=out_specs, check_vma=False)
```

```python
import functools

import jax
import jax.numpy as jnp
from jax import lax
from jax.experimental import pallas as pl
from jax.experimental.pallas import tpu as pltpu
from jax.sharding import PartitionSpec as P

huber_delta = 0.05
norm_eps = 1e-06
CORES = 2
LANES = 128
PARTS = 3
REVERSED = (1, 3)
F32 = jnp.float32
BF16 = jnp.bfloat16
VMEM = pl.BlockSpec(memory_space=pltpu.VMEM)
SMEM = pl.BlockSpec(memory_space=pltpu.SMEM)
HBM = pl.BlockSpec(memory_space=pltpu.HBM)
NT = (((1,), (1,)), ((), ()))


def round_up(value, unit):
    return -(-value // unit) * unit


def params(mib):
    return pltpu.CompilerParams(vmem_limit_bytes=mib * 1024 * 1024)


def prepare_kernel(
    per_peer,
    counts_hbm,
    table_hbm,
    map_hbm,
    teacher_hbm,
    hidden_hbm,
    projection_hbm,
    out_ref,
    student_ref,
    unit_ref,
    inverse_ref,
    counts,
    table,
    fields,
    teacher,
    hidden,
    projection,
    sems,
):
    part = projection.shape[0] // PARTS
    copies = [
        pltpu.make_async_copy(source, target, sems.at[i])
        for i, (source, target) in enumerate(
            (
                (counts_hbm, counts),
                (table_hbm, table),
                (map_hbm, fields),
                (teacher_hbm, teacher),
                (hidden_hbm, hidden),
            )
            + tuple(
                (projection_hbm.at[pl.ds(p, part)], projection.at[pl.ds(p, part)])
                for p in range(0, projection.shape[0], part)
            )
        )
    ]
    for copy in copies:
        copy.start()
    for copy in copies[:4]:
        copy.wait()
    tubes = teacher.shape[0]
    rows = fields.shape[0] // 3
    out_ref[0:tubes, :] = teacher[...]
    tube, cell, level = (fields[f * rows : (f + 1) * rows, :] for f in range(3))
    weight = jnp.zeros((rows, LANES), F32)
    for i in range(table.shape[0]):
        weight = jnp.where(level == i, table[i], weight)
    row = lax.broadcasted_iota(jnp.int32, (rows, LANES), 0)
    lane = lax.broadcasted_iota(jnp.int32, (rows, LANES), 1)
    receiver = row * (LANES // per_peer) + lane // per_peer
    count = jnp.zeros((rows, LANES), jnp.int32)
    for i in range(counts.shape[0]):
        count = jnp.where(receiver == i, counts[i], count)
    weight = jnp.where(lane % per_peer < count, weight, 0.0)
    block = jnp.concatenate([tube.astype(F32), cell.astype(F32), weight], axis=1)
    out_ref[tubes:, 0 : 3 * LANES] = block.astype(BF16)
    out_ref[tubes:, 3 * LANES :] = jnp.zeros((rows, out_ref.shape[1] - 3 * LANES), BF16)
    copies[4].wait()
    proj = jnp.zeros((hidden.shape[0], projection.shape[1]), F32)
    for i, copy in enumerate(copies[5:]):
        copy.wait()
        proj = proj + jnp.dot(
            hidden[:, i * part : (i + 1) * part],
            projection[i * part : (i + 1) * part, :],
            preferred_element_type=F32,
        )
    inverse = lax.rsqrt(jnp.sum(proj * proj, axis=1, keepdims=True) + norm_eps)
    unit = proj * inverse
    unit_ref[...] = unit
    inverse_ref[...] = jnp.broadcast_to(inverse, inverse_ref.shape)
    student_ref[...] = unit.astype(BF16)


def prepare(hidden, projection, teacher, block_map, block_counts, interp_weights):
    tubes, width = teacher.shape
    tokens = hidden.shape[0]
    slots = block_map.shape[2]
    peers = block_counts.shape[1]
    rows = slots // LANES
    return pl.pallas_call(
        functools.partial(prepare_kernel, slots // peers),
        out_shape=(
            jax.ShapeDtypeStruct((tubes + rows, width), BF16),
            jax.ShapeDtypeStruct((tokens, width), BF16),
            jax.ShapeDtypeStruct((tokens, width), F32),
            jax.ShapeDtypeStruct((tokens, LANES), F32),
        ),
        in_specs=[HBM] * 6,
        out_specs=(VMEM,) * 4,
        scratch_shapes=[
            pltpu.SMEM((peers,), jnp.int32),
            pltpu.SMEM(interp_weights.shape, F32),
            pltpu.VMEM((3 * rows, LANES), jnp.int32),
            pltpu.VMEM(teacher.shape, BF16),
            pltpu.VMEM(hidden.shape, BF16),
            pltpu.VMEM(projection.shape, BF16),
            pltpu.SemaphoreType.DMA((5 + PARTS,)),
        ],
        compiler_params=params(40),
    )(
        *(
            pltpu.with_memory_space_constraint(x, pltpu.HBM)
            for x in (
                block_counts.reshape(peers),
                interp_weights,
                block_map.reshape(3 * rows, LANES),
                teacher,
                hidden,
                projection,
            )
        )
    )


def pick(slots, window, per_peer, masks):
    shift = (LANES - window * per_peer) % LANES
    lane = lax.broadcasted_iota(jnp.int32, (slots.shape[0], LANES), 1)
    fields = []
    for f in range(3):
        part = pltpu.roll(slots[:, f * LANES : (f + 1) * LANES], shift, 1)
        part = jnp.where(lane < per_peer, part, 0.0)
        step = per_peer
        while step < LANES:
            part = part + pltpu.roll(part, step, 1)
            step *= 2
        fields.append(part)
    return [
        [jnp.sum(jnp.where(mask, part, 0.0), axis=0, keepdims=True) for part in fields]
        for mask in masks
    ]


def target_kernel(tubes, per_peer, tokens, n_held, first, n_last, dests_ref, *refs):
    held = refs[:n_held]
    outs = refs[n_held + (0 if first else 1) : -3]
    teacher, table, matrix = refs[-3:]
    group = LANES // per_peer
    depth = round_up(group * tubes, LANES)
    rows = tubes + table.shape[1]
    count = matrix.shape[0] // tokens
    groups = matrix.shape[1] // depth
    s = 0
    for h in held:
        for at in range(0, h.shape[0], rows):
            base = s // group * depth + s % group * tubes
            teacher[base : base + tubes, :] = h[at : at + tubes, :]
            slots = h[at + tubes : at + rows, 0 : 3 * LANES].astype(F32)
            for q in range(rows - tubes):
                table[s // 8, q, s % 8 : s % 8 + 1, :] = slots[q : q + 1, :]
            s += 1
    pad = depth - group * tubes
    if pad:
        for g in range(groups):
            teacher[(g + 1) * depth - pad : (g + 1) * depth, :] = jnp.zeros(
                (pad, teacher.shape[1]), BF16
            )
    sender = lax.broadcasted_iota(jnp.int32, (8, LANES), 0)
    lane = lax.broadcasted_iota(jnp.int32, (8, LANES), 1)
    masks = [sender == lane // per_peer + at for at in range(0, 8, group)]
    offset = (lax.broadcasted_iota(jnp.int32, (1, LANES), 1) // per_peer * tubes).astype(F32)
    cells = lax.broadcasted_iota(jnp.int32, (tokens, LANES), 0).astype(F32)
    places = lax.broadcasted_iota(jnp.int32, (depth, LANES), 0).astype(F32)
    for i in range(count):
        dest = dests_ref[i]
        picked = []
        for e in range(table.shape[0]):
            picked += pick(table[e, dest // group], dest % group, per_peer, masks)
        for g in range(groups):
            tube, cell, weight = picked[g]
            left = jnp.where(cells == cell, 1.0, 0.0).astype(BF16)
            right = jnp.where(places == tube + offset, weight, 0.0).astype(BF16)
            block = lax.dot_general(left, right, NT, preferred_element_type=F32)
            matrix[i * tokens : (i + 1) * tokens, g * depth : (g + 1) * depth] = block.astype(BF16)
    total = jnp.dot(matrix[...], teacher[...], preferred_element_type=F32)
    if not first:
        total = total + refs[n_held][...]
    if n_last is None:
        outs[0][...] = total
        return
    total = total * lax.rsqrt(jnp.sum(total * total, axis=1, keepdims=True) + norm_eps)
    outs[0][...] = total[0:n_last, :].astype(BF16)
    outs[1][...] = total[n_last:, :].astype(BF16)


def add_targets(total, held, dests, tubes, per_peer, tokens, rows, n_last):
    width = held[0].shape[1]
    group = LANES // per_peer
    senders = sum(h.shape[0] for h in held) // rows
    groups = senders // group
    depth = round_up(group * tubes, LANES)
    count = dests.shape[0]
    first = total is None
    extra = () if first else (total,)
    if n_last is None:
        out_shape = jax.ShapeDtypeStruct((count * tokens, width), F32)
        out_specs = VMEM
    else:
        out_shape = tuple(
            jax.ShapeDtypeStruct((n, width), BF16) for n in (n_last, count * tokens - n_last)
        )
        out_specs = (VMEM, VMEM)
    return pl.pallas_call(
        functools.partial(target_kernel, tubes, per_peer, tokens, len(held), first, n_last),
        out_shape=out_shape,
        in_specs=[SMEM] + [VMEM] * (len(held) + len(extra)),
        out_specs=out_specs,
        scratch_shapes=[
            pltpu.VMEM((groups * depth, width), BF16),
            pltpu.VMEM((-(-senders // 8), rows - tubes, 8, 3 * LANES), F32),
            pltpu.VMEM((count * tokens, groups * depth), BF16),
        ],
        input_output_aliases={} if first or n_last else {1 + len(held): 0},
        compiler_params=params(40),
    )(dests, *held, *extra)


def relation_kernel(tokens, n_rows, n_columns, last, *refs):
    students = refs[:n_rows]
    columns = refs[n_rows : n_rows + n_columns]
    teacher_ref, own_ref, column_ref = refs[n_rows + n_columns : n_rows + n_columns + 3]
    rest = refs[n_rows + n_columns + 3 : -3]
    student, column_s, column_t = refs[-3:]
    for blocks, target in ((students, student), (columns, column_s)):
        at = 0
        for block in blocks:
            target[at : at + block.shape[0], :] = block[...]
            at += block.shape[0]
    column_t[0:tokens, :] = own_ref[0:tokens, :]
    column_t[tokens:, :] = column_ref[...]
    gram_s = lax.dot_general(column_s[...], student[...], NT, preferred_element_type=F32)
    gram_t = lax.dot_general(column_t[...], teacher_ref[...], NT, preferred_element_type=F32)
    slope = jnp.clip((gram_s - gram_t) / huber_delta, -1.0, 1.0).astype(BF16)
    grad = jnp.dot(slope, student[...], preferred_element_type=F32)
    if not last:
        rest[0][...] = grad
        return
    grad = grad + rest[0][...]
    rest[1][...] = grad[0:tokens, :]
    for j, out in enumerate(rest[2:]):
        out[...] = grad[(j + 1) * tokens : (j + 2) * tokens, :].astype(BF16)


def relate(tokens, students, columns, teacher, own, column_teacher, partial):
    width = students[0].shape[1]
    total = sum(c.shape[0] for c in columns)
    n_col = total // tokens
    last = partial is not None
    if last:
        out_shape = (jax.ShapeDtypeStruct((tokens, width), F32),) + (
            jax.ShapeDtypeStruct((tokens, width), BF16),
        ) * (n_col - 1)
        out_specs = (VMEM,) * n_col
        extra = (partial,)
    else:
        out_shape = jax.ShapeDtypeStruct((total, width), F32)
        out_specs = VMEM
        extra = ()
    return pl.pallas_call(
        functools.partial(relation_kernel, tokens, len(students), len(columns), last),
        out_shape=out_shape,
        in_specs=[VMEM] * (len(students) + len(columns) + 3 + len(extra)),
        out_specs=out_specs,
        scratch_shapes=[
            pltpu.VMEM((sum(x.shape[0] for x in students), width), BF16),
            pltpu.VMEM((total, width), BF16),
            pltpu.VMEM((total, width), BF16),
        ],
        compiler_params=params(40),
    )(*students, *columns, teacher, own, column_teacher, *extra)


def finish_kernel(unit_ref, inverse_ref, projection_ref, own_ref, *refs):
    grad = own_ref[...]
    for other in refs[:-1]:
        grad = grad + other[...].astype(F32)
    grad = 2.0 * grad
    unit = unit_ref[...]
    along = jnp.sum(unit * grad, axis=1, keepdims=True)
    grad_proj = ((grad - unit * along) * inverse_ref[:, 0:1]).astype(BF16)
    refs[-1][...] = lax.dot_general(
        grad_proj, projection_ref[...], NT, preferred_element_type=F32
    ).astype(BF16)


def finish(unit, inverse, projection, own, others):
    return pl.pallas_call(
        finish_kernel,
        out_shape=jax.ShapeDtypeStruct((unit.shape[0], projection.shape[0]), BF16),
        in_specs=[VMEM] * (4 + len(others)),
        out_specs=VMEM,
        compiler_params=params(16),
    )(unit, inverse, projection, own, *others)


def join_kernel(*refs):
    at = 0
    for ref in refs[:-1]:
        refs[-1][at : at + ref.shape[0], :] = ref[...]
        at += ref.shape[0]


def join(*held):
    rows = sum(h.shape[0] for h in held)
    return pl.pallas_call(
        join_kernel,
        out_shape=jax.ShapeDtypeStruct((rows, held[0].shape[1]), held[0].dtype),
        in_specs=[VMEM] * len(held),
        out_specs=VMEM,
        compiler_params=params(8),
    )(*held)


def doubled(held, exchange, steps):
    for step in steps:
        if len(held) > 1:
            held = [join(*held)]
        held.append(exchange(held[0], step))
    return held


def local(n_row, n_col, student_hidden, projection, teacher, block_map, block_counts, interp_weights):
    tubes = teacher.shape[0]
    tokens = student_hidden.shape[0]
    per_peer = block_map.shape[2] // block_counts.shape[1]
    n_z = n_col // CORES
    row, col = lax.axis_index("row"), lax.axis_index("col")
    row_steps = [1 << b for b in range(n_row.bit_length() - 1)]
    z_steps = [1 << b for b in range(n_z.bit_length() - 1)]

    def along_row(x, k):
        return lax.ppermute(x, "row", [(i, i ^ k) for i in range(n_row)])

    def along_z(x, k):
        return lax.ppermute(x, "col", [(i, i ^ (CORES * k)) for i in range(n_col)])

    def to_partner(x):
        return lax.ppermute(x, "col", [(i, i ^ 1) for i in range(n_col)])

    payload, student, unit, inverse = prepare(
        student_hidden, projection, teacher, block_map, block_counts, interp_weights
    )
    rows = payload.shape[0]
    planes = [payload] + [along_z(payload, k) for k in range(1, n_z)]
    columns = doubled([student], along_row, row_steps)
    students = doubled([student], along_z, z_steps)
    partner_students = [to_partner(x) for x in students]
    dests = jnp.stack(
        [row * n_col + (col ^ (CORES * k)) for k in range(n_z)]
        + [(row ^ j) * n_col + col for j in range(1, n_row)]
    ).astype(jnp.int32)
    total = None
    sequence = list(range(n_z))
    if n_z > 99:
        sequence[1:3] = 2, 1
    for k in sequence:
        order = row_steps[::-1] if k in REVERSED else row_steps
        held = doubled([planes[k]], along_row, order)
        held = held + [to_partner(x) for x in held]
        n_last = n_z * tokens if k == n_z - 1 else None
        total = add_targets(total, held, dests, tubes, per_peer, tokens, rows, n_last)
    own, column = total
    partner = to_partner(own)
    grad = relate(tokens, students, columns, own, own, column, None)
    mine, *others = relate(tokens, partner_students, columns, partner, own, column, grad)
    arrived = [along_row(x, j) for j, x in enumerate(others, 1)]
    return finish(unit, inverse, projection, mine, arrived)


def solution(mesh):
    in_specs = (
        P(("row", "col"), None),
        P(),
        P(("row", "col"), None),
        P(("row", "col"), None, None),
        P(("row", "col"), None),
        P(),
    )
    out_specs = P(("row", "col"), None)
    body = functools.partial(local, mesh.shape["row"], mesh.shape["col"])
    return jax.shard_map(body, mesh=mesh, in_specs=in_specs, out_specs=out_specs, check_vma=False)
```

```python
import functools

import jax
import jax.numpy as jnp
from jax import lax
from jax.experimental import pallas as pl
from jax.experimental.pallas import tpu as pltpu
from jax.sharding import PartitionSpec as P

huber_delta = 0.05
norm_eps = 1e-06
CORES = 2
LANES = 128
PARTS = 3
REVERSED = (1, 3)
F32 = jnp.float32
BF16 = jnp.bfloat16
VMEM = pl.BlockSpec(memory_space=pltpu.VMEM)
SMEM = pl.BlockSpec(memory_space=pltpu.SMEM)
HBM = pl.BlockSpec(memory_space=pltpu.HBM)
NT = (((1,), (1,)), ((), ()))


def round_up(value, unit):
    return -(-value // unit) * unit


def params(mib):
    return pltpu.CompilerParams(vmem_limit_bytes=mib * 1024 * 1024)


def in_hbm(*arrays):
    return [pltpu.with_memory_space_constraint(x, pltpu.HBM) for x in arrays]


def started(sources, targets, sems):
    copies = [
        pltpu.make_async_copy(source, target, sems.at[i])
        for i, (source, target) in enumerate(zip(sources, targets))
    ]
    for copy in copies:
        copy.start()
    return copies


def pack_kernel(per_peer, *refs):
    out_ref, counts, table, fields, teacher, sems = refs[4:]
    for copy in started(refs[:4], (counts, table, fields, teacher), sems):
        copy.wait()
    tubes = teacher.shape[0]
    rows = fields.shape[0] // 3
    out_ref[0:tubes, :] = teacher[...]
    tube, cell, level = (fields[f * rows : (f + 1) * rows, :] for f in range(3))
    weight = jnp.zeros((rows, LANES), F32)
    for i in range(table.shape[0]):
        weight = jnp.where(level == i, table[i], weight)
    row = lax.broadcasted_iota(jnp.int32, (rows, LANES), 0)
    lane = lax.broadcasted_iota(jnp.int32, (rows, LANES), 1)
    receiver = row * (LANES // per_peer) + lane // per_peer
    count = jnp.zeros((rows, LANES), jnp.int32)
    for i in range(counts.shape[0]):
        count = jnp.where(receiver == i, counts[i], count)
    weight = jnp.where(lane % per_peer < count, weight, 0.0)
    block = jnp.concatenate([tube.astype(F32), cell.astype(F32), weight], axis=1)
    out_ref[tubes:, 0 : 3 * LANES] = block.astype(BF16)
    out_ref[tubes:, 3 * LANES :] = jnp.zeros((rows, out_ref.shape[1] - 3 * LANES), BF16)


def pack(teacher, block_map, block_counts, interp_weights):
    tubes, width = teacher.shape
    slots = block_map.shape[2]
    peers = block_counts.shape[1]
    rows = slots // LANES
    return pl.pallas_call(
        functools.partial(pack_kernel, slots // peers),
        out_shape=jax.ShapeDtypeStruct((tubes + rows, width), BF16),
        in_specs=[HBM] * 4,
        out_specs=VMEM,
        scratch_shapes=[
            pltpu.SMEM((peers,), jnp.int32),
            pltpu.SMEM(interp_weights.shape, F32),
            pltpu.VMEM((3 * rows, LANES), jnp.int32),
            pltpu.VMEM(teacher.shape, BF16),
            pltpu.SemaphoreType.DMA((4,)),
        ],
        compiler_params=params(8),
    )(
        *in_hbm(
            block_counts.reshape(peers),
            interp_weights,
            block_map.reshape(3 * rows, LANES),
            teacher,
        )
    )


def project_kernel(hidden_hbm, projection_hbm, student_ref, unit_ref, inverse_ref, hidden, projection, sems):
    part = projection.shape[0] // PARTS
    spans = [pl.ds(i * part, part) for i in range(PARTS)]
    copies = started(
        [hidden_hbm] + [projection_hbm.at[span] for span in spans],
        [hidden] + [projection.at[span] for span in spans],
        sems,
    )
    copies[0].wait()
    proj = jnp.zeros((hidden.shape[0], projection.shape[1]), F32)
    for i, copy in enumerate(copies[1:]):
        copy.wait()
        proj = proj + jnp.dot(
            hidden[:, i * part : (i + 1) * part],
            projection[i * part : (i + 1) * part, :],
            preferred_element_type=F32,
        )
    inverse = lax.rsqrt(jnp.sum(proj * proj, axis=1, keepdims=True) + norm_eps)
    unit = proj * inverse
    unit_ref[...] = unit
    inverse_ref[...] = jnp.broadcast_to(inverse, inverse_ref.shape)
    student_ref[...] = unit.astype(BF16)


def project(hidden, projection):
    tokens, width = hidden.shape[0], projection.shape[1]
    return pl.pallas_call(
        project_kernel,
        out_shape=(
            jax.ShapeDtypeStruct((tokens, width), BF16),
            jax.ShapeDtypeStruct((tokens, width), F32),
            jax.ShapeDtypeStruct((tokens, LANES), F32),
        ),
        in_specs=[HBM] * 2,
        out_specs=(VMEM,) * 3,
        scratch_shapes=[
            pltpu.VMEM(hidden.shape, BF16),
            pltpu.VMEM(projection.shape, BF16),
            pltpu.SemaphoreType.DMA((1 + PARTS,)),
        ],
        compiler_params=params(16),
    )(*in_hbm(hidden, projection))


def pick(slots, window, per_peer, masks):
    shift = (LANES - window * per_peer) % LANES
    lane = lax.broadcasted_iota(jnp.int32, (slots.shape[0], LANES), 1)
    fields = []
    for f in range(3):
        part = pltpu.roll(slots[:, f * LANES : (f + 1) * LANES], shift, 1)
        part = jnp.where(lane < per_peer, part, 0.0)
        step = per_peer
        while step < LANES:
            part = part + pltpu.roll(part, step, 1)
            step *= 2
        fields.append(part)
    return [
        [jnp.sum(jnp.where(mask, part, 0.0), axis=0, keepdims=True) for part in fields]
        for mask in masks
    ]


def target_kernel(tubes, per_peer, tokens, n_held, first, n_last, dests_ref, *refs):
    held = refs[:n_held]
    outs = refs[n_held + (0 if first else 1) : -3]
    teacher, table, matrix = refs[-3:]
    group = LANES // per_peer
    depth = round_up(group * tubes, LANES)
    rows = tubes + table.shape[1]
    count = matrix.shape[0] // tokens
    groups = matrix.shape[1] // depth
    s = 0
    for h in held:
        for at in range(0, h.shape[0], rows):
            base = s // group * depth + s % group * tubes
            teacher[base : base + tubes, :] = h[at : at + tubes, :]
            slots = h[at + tubes : at + rows, 0 : 3 * LANES].astype(F32)
            for q in range(rows - tubes):
                table[s // 8, q, s % 8 : s % 8 + 1, :] = slots[q : q + 1, :]
            s += 1
    pad = depth - group * tubes
    if pad:
        for g in range(groups):
            teacher[(g + 1) * depth - pad : (g + 1) * depth, :] = jnp.zeros(
                (pad, teacher.shape[1]), BF16
            )
    sender = lax.broadcasted_iota(jnp.int32, (8, LANES), 0)
    lane = lax.broadcasted_iota(jnp.int32, (8, LANES), 1)
    masks = [sender == lane // per_peer + at for at in range(0, 8, group)]
    offset = (lax.broadcasted_iota(jnp.int32, (1, LANES), 1) // per_peer * tubes).astype(F32)
    cells = lax.broadcasted_iota(jnp.int32, (tokens, LANES), 0).astype(F32)
    places = lax.broadcasted_iota(jnp.int32, (depth, LANES), 0).astype(F32)
    for i in range(count):
        dest = dests_ref[i]
        picked = []
        for e in range(table.shape[0]):
            picked += pick(table[e, dest // group], dest % group, per_peer, masks)
        for g in range(groups):
            tube, cell, weight = picked[g]
            left = jnp.where(cells == cell, 1.0, 0.0).astype(BF16)
            right = jnp.where(places == tube + offset, weight, 0.0).astype(BF16)
            block = lax.dot_general(left, right, NT, preferred_element_type=F32)
            matrix[i * tokens : (i + 1) * tokens, g * depth : (g + 1) * depth] = block.astype(BF16)
    total = jnp.dot(matrix[...], teacher[...], preferred_element_type=F32)
    if not first:
        total = total + refs[n_held][...]
    if n_last is None:
        outs[0][...] = total
        return
    total = total * lax.rsqrt(jnp.sum(total * total, axis=1, keepdims=True) + norm_eps)
    outs[0][...] = total[0:n_last, :].astype(BF16)
    outs[1][...] = total[n_last:, :].astype(BF16)


def add_targets(total, held, dests, tubes, per_peer, tokens, rows, n_last):
    width = held[0].shape[1]
    group = LANES // per_peer
    senders = sum(h.shape[0] for h in held) // rows
    groups = senders // group
    depth = round_up(group * tubes, LANES)
    count = dests.shape[0]
    first = total is None
    extra = () if first else (total,)
    if n_last is None:
        out_shape = jax.ShapeDtypeStruct((count * tokens, width), F32)
        out_specs = VMEM
    else:
        out_shape = tuple(
            jax.ShapeDtypeStruct((n, width), BF16) for n in (n_last, count * tokens - n_last)
        )
        out_specs = (VMEM, VMEM)
    return pl.pallas_call(
        functools.partial(target_kernel, tubes, per_peer, tokens, len(held), first, n_last),
        out_shape=out_shape,
        in_specs=[SMEM] + [VMEM] * (len(held) + len(extra)),
        out_specs=out_specs,
        scratch_shapes=[
            pltpu.VMEM((groups * depth, width), BF16),
            pltpu.VMEM((-(-senders // 8), rows - tubes, 8, 3 * LANES), F32),
            pltpu.VMEM((count * tokens, groups * depth), BF16),
        ],
        input_output_aliases={} if first or n_last else {1 + len(held): 0},
        compiler_params=params(40),
    )(dests, *held, *extra)


def relation_kernel(tokens, n_rows, starts, last, *refs):
    students = refs[:n_rows]
    columns_ref, teacher_ref = refs[n_rows : n_rows + 2]
    teachers = refs[n_rows + 2 : n_rows + 2 + len(starts)]
    rest = refs[n_rows + 2 + len(starts) : -2]
    student, column_t = refs[-2:]
    at = 0
    for block in students:
        student[at : at + block.shape[0], :] = block[...]
        at += block.shape[0]
    at = 0
    for block, (start, rows) in zip(teachers, starts):
        column_t[at : at + rows, :] = block[start : start + rows, :]
        at += rows
    gram_s = lax.dot_general(columns_ref[...], student[...], NT, preferred_element_type=F32)
    gram_t = lax.dot_general(column_t[...], teacher_ref[...], NT, preferred_element_type=F32)
    slope = jnp.clip((gram_s - gram_t) / huber_delta, -1.0, 1.0).astype(BF16)
    grad = jnp.dot(slope, student[...], preferred_element_type=F32)
    if not last:
        rest[0][...] = grad
        return
    grad = grad + rest[0][...]
    for j, out in enumerate(rest[1:]):
        out[...] = grad[j * tokens : (j + 1) * tokens, :].astype(out.dtype)


def relate(tokens, students, columns, teacher, column_teacher, partial, kinds):
    width = columns.shape[1]
    total = columns.shape[0]
    starts = tuple((start, rows) for _, start, rows in column_teacher)
    last = partial is not None
    if last:
        out_shape = tuple(jax.ShapeDtypeStruct((tokens, width), kind) for kind in kinds)
        out_specs = (VMEM,) * len(kinds)
        extra = (partial,)
    else:
        out_shape = jax.ShapeDtypeStruct((total, width), F32)
        out_specs = VMEM
        extra = ()
    return pl.pallas_call(
        functools.partial(relation_kernel, tokens, len(students), starts, last),
        out_shape=out_shape,
        in_specs=[VMEM] * (len(students) + 2 + len(starts) + len(extra)),
        out_specs=out_specs,
        scratch_shapes=[
            pltpu.VMEM((sum(x.shape[0] for x in students), width), BF16),
            pltpu.VMEM((total, width), BF16),
        ],
        compiler_params=params(40),
    )(*students, columns, teacher, *(array for array, _, _ in column_teacher), *extra)


def finish_kernel(unit_ref, inverse_ref, projection_ref, own_ref, *refs):
    out_hbm, out, sems = refs[-3:]
    grad = own_ref[...]
    for other in refs[:-3]:
        grad = grad + other[...].astype(F32)
    grad = 2.0 * grad
    unit = unit_ref[...]
    along = jnp.sum(unit * grad, axis=1, keepdims=True)
    grad_proj = ((grad - unit * along) * inverse_ref[:, 0:1]).astype(BF16)
    part = out.shape[1] // PARTS
    copies = []
    for i in range(PARTS):
        span = pl.ds(i * part, part)
        out[:, i * part : (i + 1) * part] = lax.dot_general(
            grad_proj,
            projection_ref[i * part : (i + 1) * part, :],
            NT,
            preferred_element_type=F32,
        ).astype(BF16)
        copies.append(
            pltpu.make_async_copy(out.at[:, span], out_hbm.at[:, span], sems.at[i])
        )
        copies[-1].start()
    for copy in copies:
        copy.wait()


def finish(unit, inverse, projection, own, others):
    shape = (unit.shape[0], projection.shape[0])
    return pl.pallas_call(
        finish_kernel,
        out_shape=jax.ShapeDtypeStruct(shape, BF16),
        in_specs=[VMEM] * (4 + len(others)),
        out_specs=HBM,
        scratch_shapes=[pltpu.VMEM(shape, BF16), pltpu.SemaphoreType.DMA((PARTS,))],
        compiler_params=params(16),
    )(unit, inverse, projection, own, *others)


def join_kernel(*refs):
    at = 0
    for ref in refs[:-1]:
        refs[-1][at : at + ref.shape[0], :] = ref[...]
        at += ref.shape[0]


def join(*held):
    rows = sum(h.shape[0] for h in held)
    return pl.pallas_call(
        join_kernel,
        out_shape=jax.ShapeDtypeStruct((rows, held[0].shape[1]), held[0].dtype),
        in_specs=[VMEM] * len(held),
        out_specs=VMEM,
        compiler_params=params(8),
    )(*held)


def doubled(held, exchange, steps):
    for step in steps:
        if len(held) > 1:
            held = [join(*held)]
        held.append(exchange(held[0], step))
    return held


def local(n_row, n_col, student_hidden, projection, teacher, block_map, block_counts, interp_weights):
    tubes = teacher.shape[0]
    tokens = student_hidden.shape[0]
    per_peer = block_map.shape[2] // block_counts.shape[1]
    n_z = n_col // CORES
    row, col = lax.axis_index("row"), lax.axis_index("col")
    row_steps = [1 << b for b in range(n_row.bit_length() - 1)]
    z_steps = [1 << b for b in range(n_z.bit_length() - 1)]

    def along_row(x, k):
        return lax.ppermute(x, "row", [(i, i ^ k) for i in range(n_row)])

    def along_z(x, k):
        return lax.ppermute(x, "col", [(i, i ^ (CORES * k)) for i in range(n_col)])

    def to_partner(x):
        return lax.ppermute(x, "col", [(i, i ^ 1) for i in range(n_col)])

    payload = pack(teacher, block_map, block_counts, interp_weights)
    student, unit, inverse = project(student_hidden, projection)
    rows = payload.shape[0]
    planes = [payload] + [along_z(payload, k) for k in range(1, n_z)]
    columns = doubled([student], along_row, row_steps[::-1])
    students = doubled([student], along_z, z_steps)
    partner_students = [to_partner(x) for x in students]
    offsets = [0]
    for step in row_steps[::-1]:
        offsets += [j ^ step for j in offsets]
    dests = jnp.stack(
        [row * n_col + (col ^ (CORES * k)) for k in range(n_z)]
        + [(row ^ j) * n_col + col for j in offsets[1:]]
    ).astype(jnp.int32)
    total = None
    batches = [[k] for k in range(min(n_z, 2))] + [
        list(range(k, min(k + 2, n_z))) for k in range(2, n_z, 2)
    ]
    for batch in batches:
        senders = []
        for k in batch:
            order = row_steps[::-1] if k in REVERSED else row_steps
            held = doubled([planes[k]], along_row, order)
            senders += held
            senders += [to_partner(x) for x in held]
        n_last = n_z * tokens if batch is batches[-1] else None
        total = add_targets(total, senders, dests, tubes, per_peer, tokens, rows, n_last)
    own, column = total
    partner = to_partner(own)
    half = n_row // 2
    near = ((own, 0, tokens), (column, 0, (half - 1) * tokens))
    far = ((column, (half - 1) * tokens, half * tokens),)
    near_kinds = (F32,) + (BF16,) * (half - 1)
    far_kinds = (BF16,) * half
    sides = ((columns[0], near, near_kinds), (columns[1], far, far_kinds))
    sums = [
        relate(tokens, students, c, own, t, None, kinds)
        for c, t, kinds in sides
    ]
    blocks = []
    for i, (c, t, kinds) in enumerate(sides):
        blocks += relate(tokens, partner_students, c, partner, t, sums[i], kinds)
    arrived = [along_row(x, j) for j, x in zip(offsets[1:], blocks[1:])]
    return finish(unit, inverse, projection, blocks[0], arrived)


def solution(mesh):
    in_specs = (
        P(("row", "col"), None),
        P(),
        P(("row", "col"), None),
        P(("row", "col"), None, None),
        P(("row", "col"), None),
        P(),
    )
    out_specs = P(("row", "col"), None)
    body = functools.partial(local, mesh.shape["row"], mesh.shape["col"])
    return jax.shard_map(body, mesh=mesh, in_specs=in_specs, out_specs=out_specs, check_vma=False)
```

```python
import functools

import jax
import jax.numpy as jnp
from jax import lax
from jax.experimental import pallas as pl
from jax.experimental.pallas import tpu as pltpu
from jax.sharding import PartitionSpec as P

huber_delta = 0.05
norm_eps = 1e-06
CORES = 2
LANES = 128
PARTS = 3
REVERSED = (1, 3)
F32 = jnp.float32
BF16 = jnp.bfloat16
VMEM = pl.BlockSpec(memory_space=pltpu.VMEM)
SMEM = pl.BlockSpec(memory_space=pltpu.SMEM)
HBM = pl.BlockSpec(memory_space=pltpu.HBM)
NT = (((1,), (1,)), ((), ()))


def round_up(value, unit):
    return -(-value // unit) * unit


def params(mib):
    return pltpu.CompilerParams(vmem_limit_bytes=mib * 1024 * 1024)


def in_hbm(*arrays):
    return [pltpu.with_memory_space_constraint(x, pltpu.HBM) for x in arrays]


def started(sources, targets, sems):
    copies = [
        pltpu.make_async_copy(source, target, sems.at[i])
        for i, (source, target) in enumerate(zip(sources, targets))
    ]
    for copy in copies:
        copy.start()
    return copies


def pack_kernel(per_peer, *refs):
    out_ref, counts, table, fields, teacher, sems = refs[4:]
    for copy in started(refs[:4], (counts, table, fields, teacher), sems):
        copy.wait()
    tubes = teacher.shape[0]
    rows = fields.shape[0] // 3
    out_ref[0:tubes, :] = teacher[...]
    tube, cell, level = (fields[f * rows : (f + 1) * rows, :] for f in range(3))
    weight = jnp.zeros((rows, LANES), F32)
    for i in range(table.shape[0]):
        weight = jnp.where(level == i, table[i], weight)
    row = lax.broadcasted_iota(jnp.int32, (rows, LANES), 0)
    lane = lax.broadcasted_iota(jnp.int32, (rows, LANES), 1)
    receiver = row * (LANES // per_peer) + lane // per_peer
    count = jnp.zeros((rows, LANES), jnp.int32)
    for i in range(counts.shape[0]):
        count = jnp.where(receiver == i, counts[i], count)
    weight = jnp.where(lane % per_peer < count, weight, 0.0)
    block = jnp.concatenate([tube.astype(F32), cell.astype(F32), weight], axis=1)
    out_ref[tubes:, 0 : 3 * LANES] = block.astype(BF16)
    out_ref[tubes:, 3 * LANES :] = jnp.zeros((rows, out_ref.shape[1] - 3 * LANES), BF16)


def pack(teacher, block_map, block_counts, interp_weights):
    tubes, width = teacher.shape
    slots = block_map.shape[2]
    peers = block_counts.shape[1]
    rows = slots // LANES
    return pl.pallas_call(
        functools.partial(pack_kernel, slots // peers),
        out_shape=jax.ShapeDtypeStruct((tubes + rows, width), BF16),
        in_specs=[HBM] * 4,
        out_specs=VMEM,
        scratch_shapes=[
            pltpu.SMEM((peers,), jnp.int32),
            pltpu.SMEM(interp_weights.shape, F32),
            pltpu.VMEM((3 * rows, LANES), jnp.int32),
            pltpu.VMEM(teacher.shape, BF16),
            pltpu.SemaphoreType.DMA((4,)),
        ],
        compiler_params=params(8),
    )(
        *in_hbm(
            block_counts.reshape(peers),
            interp_weights,
            block_map.reshape(3 * rows, LANES),
            teacher,
        )
    )


def project_kernel(hidden_hbm, projection_hbm, student_ref, unit_ref, inverse_ref, hidden, projection, sems):
    part = projection.shape[0] // PARTS
    spans = [pl.ds(i * part, part) for i in range(PARTS)]
    copies = started(
        [hidden_hbm] + [projection_hbm.at[span] for span in spans],
        [hidden] + [projection.at[span] for span in spans],
        sems,
    )
    copies[0].wait()
    proj = jnp.zeros((hidden.shape[0], projection.shape[1]), F32)
    for i, copy in enumerate(copies[1:]):
        copy.wait()
        proj = proj + jnp.dot(
            hidden[:, i * part : (i + 1) * part],
            projection[i * part : (i + 1) * part, :],
            preferred_element_type=F32,
        )
    inverse = lax.rsqrt(jnp.sum(proj * proj, axis=1, keepdims=True) + norm_eps)
    unit = proj * inverse
    unit_ref[...] = unit
    inverse_ref[...] = jnp.broadcast_to(inverse, inverse_ref.shape)
    student_ref[...] = unit.astype(BF16)


def project(hidden, projection):
    tokens, width = hidden.shape[0], projection.shape[1]
    return pl.pallas_call(
        project_kernel,
        out_shape=(
            jax.ShapeDtypeStruct((tokens, width), BF16),
            jax.ShapeDtypeStruct((tokens, width), F32),
            jax.ShapeDtypeStruct((tokens, LANES), F32),
        ),
        in_specs=[HBM] * 2,
        out_specs=(VMEM,) * 3,
        scratch_shapes=[
            pltpu.VMEM(hidden.shape, BF16),
            pltpu.VMEM(projection.shape, BF16),
            pltpu.SemaphoreType.DMA((1 + PARTS,)),
        ],
        compiler_params=params(16),
    )(*in_hbm(hidden, projection))


def pick(slots, window, per_peer, masks):
    shift = (LANES - window * per_peer) % LANES
    lane = lax.broadcasted_iota(jnp.int32, (slots.shape[0], LANES), 1)
    fields = []
    for f in range(3):
        part = pltpu.roll(slots[:, f * LANES : (f + 1) * LANES], shift, 1)
        part = jnp.where(lane < per_peer, part, 0.0)
        step = per_peer
        while step < LANES:
            part = part + pltpu.roll(part, step, 1)
            step *= 2
        fields.append(part)
    return [
        [jnp.sum(jnp.where(mask, part, 0.0), axis=0, keepdims=True) for part in fields]
        for mask in masks
    ]


def target_kernel(tubes, per_peer, tokens, n_held, first, n_last, dests_ref, *refs):
    held = refs[:n_held]
    outs = refs[n_held + (0 if first else 1) : -3]
    teacher, table, matrix = refs[-3:]
    group = LANES // per_peer
    depth = round_up(group * tubes, LANES)
    rows = tubes + table.shape[1]
    count = matrix.shape[0] // tokens
    groups = matrix.shape[1] // depth
    s = 0
    for h in held:
        for at in range(0, h.shape[0], rows):
            base = s // group * depth + s % group * tubes
            teacher[base : base + tubes, :] = h[at : at + tubes, :]
            slots = h[at + tubes : at + rows, 0 : 3 * LANES].astype(F32)
            for q in range(rows - tubes):
                table[s // 8, q, s % 8 : s % 8 + 1, :] = slots[q : q + 1, :]
            s += 1
    pad = depth - group * tubes
    if pad:
        for g in range(groups):
            teacher[(g + 1) * depth - pad : (g + 1) * depth, :] = jnp.zeros(
                (pad, teacher.shape[1]), BF16
            )
    sender = lax.broadcasted_iota(jnp.int32, (8, LANES), 0)
    lane = lax.broadcasted_iota(jnp.int32, (8, LANES), 1)
    masks = [sender == lane // per_peer + at for at in range(0, 8, group)]
    offset = (lax.broadcasted_iota(jnp.int32, (1, LANES), 1) // per_peer * tubes).astype(F32)
    cells = lax.broadcasted_iota(jnp.int32, (tokens, LANES), 0).astype(F32)
    places = lax.broadcasted_iota(jnp.int32, (depth, LANES), 0).astype(F32)
    for i in range(count):
        dest = dests_ref[i]
        picked = []
        for e in range(table.shape[0]):
            picked += pick(table[e, dest // group], dest % group, per_peer, masks)
        for g in range(groups):
            tube, cell, weight = picked[g]
            left = jnp.where(cells == cell, 1.0, 0.0).astype(BF16)
            right = jnp.where(places == tube + offset, weight, 0.0).astype(BF16)
            block = lax.dot_general(left, right, NT, preferred_element_type=F32)
            matrix[i * tokens : (i + 1) * tokens, g * depth : (g + 1) * depth] = block.astype(BF16)
    total = jnp.dot(matrix[...], teacher[...], preferred_element_type=F32)
    if not first:
        total = total + refs[n_held][...]
    if n_last is None:
        outs[0][...] = total
        return
    total = total * lax.rsqrt(jnp.sum(total * total, axis=1, keepdims=True) + norm_eps)
    outs[0][...] = total[0:n_last, :].astype(BF16)
    outs[1][...] = total[n_last:, :].astype(BF16)


def add_targets(total, held, dests, tubes, per_peer, tokens, rows, n_last):
    width = held[0].shape[1]
    group = LANES // per_peer
    senders = sum(h.shape[0] for h in held) // rows
    groups = senders // group
    depth = round_up(group * tubes, LANES)
    count = dests.shape[0]
    first = total is None
    extra = () if first else (total,)
    if n_last is None:
        out_shape = jax.ShapeDtypeStruct((count * tokens, width), F32)
        out_specs = VMEM
    else:
        out_shape = tuple(
            jax.ShapeDtypeStruct((n, width), BF16) for n in (n_last, count * tokens - n_last)
        )
        out_specs = (VMEM, VMEM)
    return pl.pallas_call(
        functools.partial(target_kernel, tubes, per_peer, tokens, len(held), first, n_last),
        out_shape=out_shape,
        in_specs=[SMEM] + [VMEM] * (len(held) + len(extra)),
        out_specs=out_specs,
        scratch_shapes=[
            pltpu.VMEM((groups * depth, width), BF16),
            pltpu.VMEM((-(-senders // 8), rows - tubes, 8, 3 * LANES), F32),
            pltpu.VMEM((count * tokens, groups * depth), BF16),
        ],
        input_output_aliases={} if first or n_last else {1 + len(held): 0},
        compiler_params=params(40),
    )(dests, *held, *extra)


def relation_kernel(tokens, n_rows, starts, last, *refs):
    students = refs[:n_rows]
    columns_ref, teacher_ref = refs[n_rows : n_rows + 2]
    teachers = refs[n_rows + 2 : n_rows + 2 + len(starts)]
    rest = refs[n_rows + 2 + len(starts) : -2]
    student, column_t = refs[-2:]
    at = 0
    for block in students:
        student[at : at + block.shape[0], :] = block[...]
        at += block.shape[0]
    at = 0
    for block, (start, rows) in zip(teachers, starts):
        column_t[at : at + rows, :] = block[start : start + rows, :]
        at += rows
    gram_s = lax.dot_general(columns_ref[...], student[...], NT, preferred_element_type=F32)
    gram_t = lax.dot_general(column_t[...], teacher_ref[...], NT, preferred_element_type=F32)
    slope = jnp.clip((gram_s - gram_t) / huber_delta, -1.0, 1.0).astype(BF16)
    grad = jnp.dot(slope, student[...], preferred_element_type=F32)
    if not last:
        rest[0][...] = grad
        return
    grad = grad + rest[0][...]
    for j, out in enumerate(rest[1:]):
        out[...] = grad[j * tokens : (j + 1) * tokens, :].astype(out.dtype)


def relate(tokens, students, columns, teacher, column_teacher, partial, kinds):
    width = columns.shape[1]
    total = columns.shape[0]
    starts = tuple((start, rows) for _, start, rows in column_teacher)
    last = partial is not None
    if last:
        out_shape = tuple(jax.ShapeDtypeStruct((tokens, width), kind) for kind in kinds)
        out_specs = (VMEM,) * len(kinds)
        extra = (partial,)
    else:
        out_shape = jax.ShapeDtypeStruct((total, width), F32)
        out_specs = VMEM
        extra = ()
    return pl.pallas_call(
        functools.partial(relation_kernel, tokens, len(students), starts, last),
        out_shape=out_shape,
        in_specs=[VMEM] * (len(students) + 2 + len(starts) + len(extra)),
        out_specs=out_specs,
        scratch_shapes=[
            pltpu.VMEM((sum(x.shape[0] for x in students), width), BF16),
            pltpu.VMEM((total, width), BF16),
        ],
        compiler_params=params(40),
    )(*students, columns, teacher, *(array for array, _, _ in column_teacher), *extra)


def finish_kernel(unit_ref, inverse_ref, projection_ref, own_ref, *refs):
    out_hbm, out, sems = refs[-3:]
    grad = own_ref[...]
    for other in refs[:-3]:
        grad = grad + other[...].astype(F32)
    grad = 2.0 * grad
    unit = unit_ref[...]
    along = jnp.sum(unit * grad, axis=1, keepdims=True)
    grad_proj = ((grad - unit * along) * inverse_ref[:, 0:1]).astype(BF16)
    part = out.shape[1] // PARTS
    copies = []
    for i in range(PARTS):
        span = pl.ds(i * part, part)
        out[:, i * part : (i + 1) * part] = lax.dot_general(
            grad_proj,
            projection_ref[i * part : (i + 1) * part, :],
            NT,
            preferred_element_type=F32,
        ).astype(BF16)
        copies.append(
            pltpu.make_async_copy(out.at[:, span], out_hbm.at[:, span], sems.at[i])
        )
        copies[-1].start()
    for copy in copies:
        copy.wait()


def finish(unit, inverse, projection, own, others):
    shape = (unit.shape[0], projection.shape[0])
    return pl.pallas_call(
        finish_kernel,
        out_shape=jax.ShapeDtypeStruct(shape, BF16),
        in_specs=[VMEM] * (4 + len(others)),
        out_specs=HBM,
        scratch_shapes=[pltpu.VMEM(shape, BF16), pltpu.SemaphoreType.DMA((PARTS,))],
        compiler_params=params(16),
    )(unit, inverse, projection, own, *others)


def join_kernel(*refs):
    at = 0
    for ref in refs[:-1]:
        refs[-1][at : at + ref.shape[0], :] = ref[...]
        at += ref.shape[0]


def join(*held):
    rows = sum(h.shape[0] for h in held)
    return pl.pallas_call(
        join_kernel,
        out_shape=jax.ShapeDtypeStruct((rows, held[0].shape[1]), held[0].dtype),
        in_specs=[VMEM] * len(held),
        out_specs=VMEM,
        compiler_params=params(8),
    )(*held)


def doubled(held, exchange, steps):
    for step in steps:
        if len(held) > 1:
            held = [join(*held)]
        held.append(exchange(held[0], step))
    return held


def local(n_row, n_col, student_hidden, projection, teacher, block_map, block_counts, interp_weights):
    tubes = teacher.shape[0]
    tokens = student_hidden.shape[0]
    per_peer = block_map.shape[2] // block_counts.shape[1]
    n_z = n_col // CORES
    row, col = lax.axis_index("row"), lax.axis_index("col")
    row_steps = [1 << b for b in range(n_row.bit_length() - 1)]
    z_steps = [1 << b for b in range(n_z.bit_length() - 1)]

    def along_row(x, k):
        return lax.ppermute(x, "row", [(i, i ^ k) for i in range(n_row)])

    def along_z(x, k):
        return lax.ppermute(x, "col", [(i, i ^ (CORES * k)) for i in range(n_col)])

    def to_partner(x):
        return lax.ppermute(x, "col", [(i, i ^ 1) for i in range(n_col)])

    payload = pack(teacher, block_map, block_counts, interp_weights)
    student, unit, inverse = project(student_hidden, projection)
    rows = payload.shape[0]
    planes = [payload] + [along_z(payload, k) for k in range(1, n_z)]
    columns = doubled([student], along_row, row_steps[::-1])
    students = doubled([student], along_z, z_steps)
    partner_students = [to_partner(x) for x in students]
    offsets = [0]
    for step in row_steps[::-1]:
        offsets += [j ^ step for j in offsets]
    dests = jnp.stack(
        [row * n_col + (col ^ (CORES * k)) for k in range(n_z)]
        + [(row ^ j) * n_col + col for j in offsets[1:]]
    ).astype(jnp.int32)
    total = None
    early, late = [], []
    batches = []
    for k in range(n_z):
        order = row_steps[::-1] if k in REVERSED else row_steps
        held = doubled([planes[k]], along_row, order)
        halves = [(x, to_partner(x)) for x in held]
        if k < n_z - 2:
            batches.append([*halves[0], *halves[1]])
        else:
            early += halves[0]
            late += halves[1]
    batches = batches[:-1] + [sum(batches[-1:], []) + early]
    batches.append(late)
    for i, senders in enumerate(batches):
        n_last = n_z * tokens if i == len(batches) - 1 else None
        total = add_targets(total, senders, dests, tubes, per_peer, tokens, rows, n_last)
    own, column = total
    partner = to_partner(own)
    half = n_row // 2
    near = ((own, 0, tokens), (column, 0, (half - 1) * tokens))
    far = ((column, (half - 1) * tokens, half * tokens),)
    near_kinds = (F32,) + (BF16,) * (half - 1)
    far_kinds = (BF16,) * half
    sides = ((columns[0], near, near_kinds), (columns[1], far, far_kinds))
    sums = [
        relate(tokens, students, c, own, t, None, kinds)
        for c, t, kinds in sides
    ]
    blocks = []
    for i, (c, t, kinds) in enumerate(sides):
        blocks += relate(tokens, partner_students, c, partner, t, sums[i], kinds)
    arrived = [along_row(x, j) for j, x in zip(offsets[1:], blocks[1:])]
    return finish(unit, inverse, projection, blocks[0], arrived)


def solution(mesh):
    in_specs = (
        P(("row", "col"), None),
        P(),
        P(("row", "col"), None),
        P(("row", "col"), None, None),
        P(("row", "col"), None),
        P(),
    )
    out_specs = P(("row", "col"), None)
    body = functools.partial(local, mesh.shape["row"], mesh.shape["col"])
    return jax.shard_map(body, mesh=mesh, in_specs=in_specs, out_specs=out_specs, check_vma=False)
```

```python
import functools

import jax
import jax.numpy as jnp
from jax import lax
from jax.experimental import pallas as pl
from jax.experimental.pallas import tpu as pltpu
from jax.sharding import PartitionSpec as P

huber_delta = 0.05
norm_eps = 1e-06
CORES = 2
LANES = 128
PARTS = 5
REVERSED = (1, 3)
F32 = jnp.float32
BF16 = jnp.bfloat16
VMEM = pl.BlockSpec(memory_space=pltpu.VMEM)
SMEM = pl.BlockSpec(memory_space=pltpu.SMEM)
HBM = pl.BlockSpec(memory_space=pltpu.HBM)
NT = (((1,), (1,)), ((), ()))


def round_up(value, unit):
    return -(-value // unit) * unit


def params(mib):
    return pltpu.CompilerParams(vmem_limit_bytes=mib * 1024 * 1024)


def in_hbm(*arrays):
    return [pltpu.with_memory_space_constraint(x, pltpu.HBM) for x in arrays]


def started(sources, targets, sems):
    copies = [
        pltpu.make_async_copy(source, target, sems.at[i])
        for i, (source, target) in enumerate(zip(sources, targets))
    ]
    for copy in copies:
        copy.start()
    return copies


def pack_kernel(per_peer, *refs):
    out_ref, counts, table, fields, teacher, sems = refs[4:]
    for copy in started(refs[:4], (counts, table, fields, teacher), sems):
        copy.wait()
    tubes = teacher.shape[0]
    rows = fields.shape[0] // 3
    out_ref[0:tubes, :] = teacher[...]
    tube, cell, level = (fields[f * rows : (f + 1) * rows, :] for f in range(3))
    weight = jnp.zeros((rows, LANES), F32)
    for i in range(table.shape[0]):
        weight = jnp.where(level == i, table[i], weight)
    row = lax.broadcasted_iota(jnp.int32, (rows, LANES), 0)
    lane = lax.broadcasted_iota(jnp.int32, (rows, LANES), 1)
    receiver = row * (LANES // per_peer) + lane // per_peer
    count = jnp.zeros((rows, LANES), jnp.int32)
    for i in range(counts.shape[0]):
        count = jnp.where(receiver == i, counts[i], count)
    weight = jnp.where(lane % per_peer < count, weight, 0.0)
    block = jnp.concatenate([tube.astype(F32), cell.astype(F32), weight], axis=1)
    out_ref[tubes:, 0 : 3 * LANES] = block.astype(BF16)
    out_ref[tubes:, 3 * LANES :] = jnp.zeros((rows, out_ref.shape[1] - 3 * LANES), BF16)


def pack(teacher, block_map, block_counts, interp_weights):
    tubes, width = teacher.shape
    slots = block_map.shape[2]
    peers = block_counts.shape[1]
    rows = slots // LANES
    return pl.pallas_call(
        functools.partial(pack_kernel, slots // peers),
        out_shape=jax.ShapeDtypeStruct((tubes + rows, width), BF16),
        in_specs=[HBM] * 4,
        out_specs=VMEM,
        scratch_shapes=[
            pltpu.SMEM((peers,), jnp.int32),
            pltpu.SMEM(interp_weights.shape, F32),
            pltpu.VMEM((3 * rows, LANES), jnp.int32),
            pltpu.VMEM(teacher.shape, BF16),
            pltpu.SemaphoreType.DMA((4,)),
        ],
        compiler_params=params(8),
    )(
        *in_hbm(
            block_counts.reshape(peers),
            interp_weights,
            block_map.reshape(3 * rows, LANES),
            teacher,
        )
    )


def project_kernel(hidden_hbm, projection_hbm, student_ref, unit_ref, inverse_ref, hidden, projection, sems):
    part = projection.shape[0] // PARTS
    spans = [pl.ds(i * part, part) for i in range(PARTS)]
    copies = started(
        [hidden_hbm] + [projection_hbm.at[span] for span in spans],
        [hidden] + [projection.at[span] for span in spans],
        sems,
    )
    copies[0].wait()
    proj = jnp.zeros((hidden.shape[0], projection.shape[1]), F32)
    for i, copy in enumerate(copies[1:]):
        copy.wait()
        proj = proj + jnp.dot(
            hidden[:, i * part : (i + 1) * part],
            projection[i * part : (i + 1) * part, :],
            preferred_element_type=F32,
        )
    inverse = lax.rsqrt(jnp.sum(proj * proj, axis=1, keepdims=True) + norm_eps)
    unit = proj * inverse
    unit_ref[...] = unit
    inverse_ref[...] = jnp.broadcast_to(inverse, inverse_ref.shape)
    student_ref[...] = unit.astype(BF16)


def project(hidden, projection):
    tokens, width = hidden.shape[0], projection.shape[1]
    return pl.pallas_call(
        project_kernel,
        out_shape=(
            jax.ShapeDtypeStruct((tokens, width), BF16),
            jax.ShapeDtypeStruct((tokens, width), F32),
            jax.ShapeDtypeStruct((tokens, LANES), F32),
        ),
        in_specs=[HBM] * 2,
        out_specs=(VMEM,) * 3,
        scratch_shapes=[
            pltpu.VMEM(hidden.shape, BF16),
            pltpu.VMEM(projection.shape, BF16),
            pltpu.SemaphoreType.DMA((1 + PARTS,)),
        ],
        compiler_params=params(16),
    )(*in_hbm(hidden, projection))


def pick(slots, window, per_peer, masks):
    shift = (LANES - window * per_peer) % LANES
    lane = lax.broadcasted_iota(jnp.int32, (slots.shape[0], LANES), 1)
    fields = []
    for f in range(3):
        part = pltpu.roll(slots[:, f * LANES : (f + 1) * LANES], shift, 1)
        part = jnp.where(lane < per_peer, part, 0.0)
        step = per_peer
        while step < LANES:
            part = part + pltpu.roll(part, step, 1)
            step *= 2
        fields.append(part)
    return [
        [jnp.sum(jnp.where(mask, part, 0.0), axis=0, keepdims=True) for part in fields]
        for mask in masks
    ]


def target_kernel(tubes, per_peer, tokens, n_held, first, n_last, dests_ref, *refs):
    held = refs[:n_held]
    outs = refs[n_held + (0 if first else 1) : -3]
    teacher, table, matrix = refs[-3:]
    group = LANES // per_peer
    depth = round_up(group * tubes, LANES)
    rows = tubes + table.shape[1]
    count = matrix.shape[0] // tokens
    groups = matrix.shape[1] // depth
    s = 0
    for h in held:
        for at in range(0, h.shape[0], rows):
            base = s // group * depth + s % group * tubes
            teacher[base : base + tubes, :] = h[at : at + tubes, :]
            slots = h[at + tubes : at + rows, 0 : 3 * LANES].astype(F32)
            for q in range(rows - tubes):
                table[s // 8, q, s % 8 : s % 8 + 1, :] = slots[q : q + 1, :]
            s += 1
    pad = depth - group * tubes
    if pad:
        for g in range(groups):
            teacher[(g + 1) * depth - pad : (g + 1) * depth, :] = jnp.zeros(
                (pad, teacher.shape[1]), BF16
            )
    sender = lax.broadcasted_iota(jnp.int32, (8, LANES), 0)
    lane = lax.broadcasted_iota(jnp.int32, (8, LANES), 1)
    masks = [sender == lane // per_peer + at for at in range(0, 8, group)]
    offset = (lax.broadcasted_iota(jnp.int32, (1, LANES), 1) // per_peer * tubes).astype(F32)
    cells = lax.broadcasted_iota(jnp.int32, (tokens, LANES), 0).astype(F32)
    places = lax.broadcasted_iota(jnp.int32, (depth, LANES), 0).astype(F32)
    for i in range(count):
        dest = dests_ref[i]
        picked = []
        for e in range(table.shape[0]):
            picked += pick(table[e, dest // group], dest % group, per_peer, masks)
        for g in range(groups):
            tube, cell, weight = picked[g]
            left = jnp.where(cells == cell, 1.0, 0.0).astype(BF16)
            right = jnp.where(places == tube + offset, weight, 0.0).astype(BF16)
            block = lax.dot_general(left, right, NT, preferred_element_type=F32)
            matrix[i * tokens : (i + 1) * tokens, g * depth : (g + 1) * depth] = block.astype(BF16)
    total = jnp.dot(matrix[...], teacher[...], preferred_element_type=F32)
    if not first:
        total = total + refs[n_held][...]
    if n_last is None:
        outs[0][...] = total
        return
    total = total * lax.rsqrt(jnp.sum(total * total, axis=1, keepdims=True) + norm_eps)
    outs[0][...] = total[0:n_last, :].astype(BF16)
    outs[1][...] = total[n_last:, :].astype(BF16)


def add_targets(total, held, dests, tubes, per_peer, tokens, rows, n_last):
    width = held[0].shape[1]
    group = LANES // per_peer
    senders = sum(h.shape[0] for h in held) // rows
    groups = senders // group
    depth = round_up(group * tubes, LANES)
    count = dests.shape[0]
    first = total is None
    extra = () if first else (total,)
    if n_last is None:
        out_shape = jax.ShapeDtypeStruct((count * tokens, width), F32)
        out_specs = VMEM
    else:
        out_shape = tuple(
            jax.ShapeDtypeStruct((n, width), BF16) for n in (n_last, count * tokens - n_last)
        )
        out_specs = (VMEM, VMEM)
    return pl.pallas_call(
        functools.partial(target_kernel, tubes, per_peer, tokens, len(held), first, n_last),
        out_shape=out_shape,
        in_specs=[SMEM] + [VMEM] * (len(held) + len(extra)),
        out_specs=out_specs,
        scratch_shapes=[
            pltpu.VMEM((groups * depth, width), BF16),
            pltpu.VMEM((-(-senders // 8), rows - tubes, 8, 3 * LANES), F32),
            pltpu.VMEM((count * tokens, groups * depth), BF16),
        ],
        input_output_aliases={} if first or n_last else {1 + len(held): 0},
        compiler_params=params(40),
    )(dests, *held, *extra)


def relation_kernel(tokens, n_rows, starts, last, *refs):
    students = refs[:n_rows]
    columns_ref, teacher_ref = refs[n_rows : n_rows + 2]
    teachers = refs[n_rows + 2 : n_rows + 2 + len(starts)]
    rest = refs[n_rows + 2 + len(starts) : -2]
    student, column_t = refs[-2:]
    at = 0
    for block in students:
        student[at : at + block.shape[0], :] = block[...]
        at += block.shape[0]
    at = 0
    for block, (start, rows) in zip(teachers, starts):
        column_t[at : at + rows, :] = block[start : start + rows, :]
        at += rows
    gram_s = lax.dot_general(columns_ref[...], student[...], NT, preferred_element_type=F32)
    gram_t = lax.dot_general(column_t[...], teacher_ref[...], NT, preferred_element_type=F32)
    slope = jnp.clip((gram_s - gram_t) / huber_delta, -1.0, 1.0).astype(BF16)
    grad = jnp.dot(slope, student[...], preferred_element_type=F32)
    if not last:
        rest[0][...] = grad
        return
    grad = grad + rest[0][...]
    for j, out in enumerate(rest[1:]):
        out[...] = grad[j * tokens : (j + 1) * tokens, :].astype(out.dtype)


def relate(tokens, students, columns, teacher, column_teacher, partial, kinds):
    width = columns.shape[1]
    total = columns.shape[0]
    starts = tuple((start, rows) for _, start, rows in column_teacher)
    last = partial is not None
    if last:
        out_shape = tuple(jax.ShapeDtypeStruct((tokens, width), kind) for kind in kinds)
        out_specs = (VMEM,) * len(kinds)
        extra = (partial,)
    else:
        out_shape = jax.ShapeDtypeStruct((total, width), F32)
        out_specs = VMEM
        extra = ()
    return pl.pallas_call(
        functools.partial(relation_kernel, tokens, len(students), starts, last),
        out_shape=out_shape,
        in_specs=[VMEM] * (len(students) + 2 + len(starts) + len(extra)),
        out_specs=out_specs,
        scratch_shapes=[
            pltpu.VMEM((sum(x.shape[0] for x in students), width), BF16),
            pltpu.VMEM((total, width), BF16),
        ],
        compiler_params=params(40),
    )(*students, columns, teacher, *(array for array, _, _ in column_teacher), *extra)


def finish_kernel(unit_ref, inverse_ref, projection_ref, own_ref, *refs):
    out_hbm, out, sems = refs[-3:]
    grad = own_ref[...]
    for other in refs[:-3]:
        grad = grad + other[...].astype(F32)
    grad = 2.0 * grad
    unit = unit_ref[...]
    along = jnp.sum(unit * grad, axis=1, keepdims=True)
    grad_proj = ((grad - unit * along) * inverse_ref[:, 0:1]).astype(BF16)
    part = out.shape[1] // PARTS
    copies = []
    for i in range(PARTS):
        span = pl.ds(i * part, part)
        out[:, i * part : (i + 1) * part] = jnp.dot(
            grad_proj,
            projection_ref[:, i * part : (i + 1) * part],
            preferred_element_type=F32,
        ).astype(BF16)
        copies.append(
            pltpu.make_async_copy(out.at[:, span], out_hbm.at[:, span], sems.at[i])
        )
        copies[-1].start()
    for copy in copies:
        copy.wait()


def finish(unit, inverse, projection, own, others):
    shape = (unit.shape[0], projection.shape[1])
    return pl.pallas_call(
        finish_kernel,
        out_shape=jax.ShapeDtypeStruct(shape, BF16),
        in_specs=[VMEM] * (4 + len(others)),
        out_specs=HBM,
        scratch_shapes=[pltpu.VMEM(shape, BF16), pltpu.SemaphoreType.DMA((PARTS,))],
        compiler_params=params(16),
    )(unit, inverse, projection, own, *others)


def turn_kernel(in_ref, out_ref):
    out_ref[...] = in_ref[...].T


def turn(x):
    return pl.pallas_call(
        turn_kernel,
        out_shape=jax.ShapeDtypeStruct(x.shape[::-1], x.dtype),
        in_specs=[VMEM],
        out_specs=VMEM,
        compiler_params=params(16),
    )(x)


def join_kernel(*refs):
    at = 0
    for ref in refs[:-1]:
        refs[-1][at : at + ref.shape[0], :] = ref[...]
        at += ref.shape[0]


def join(*held):
    rows = sum(h.shape[0] for h in held)
    return pl.pallas_call(
        join_kernel,
        out_shape=jax.ShapeDtypeStruct((rows, held[0].shape[1]), held[0].dtype),
        in_specs=[VMEM] * len(held),
        out_specs=VMEM,
        compiler_params=params(8),
    )(*held)


def doubled(held, exchange, steps):
    for step in steps:
        if len(held) > 1:
            held = [join(*held)]
        held.append(exchange(held[0], step))
    return held


def local(n_row, n_col, student_hidden, projection, teacher, block_map, block_counts, interp_weights):
    tubes = teacher.shape[0]
    tokens = student_hidden.shape[0]
    per_peer = block_map.shape[2] // block_counts.shape[1]
    n_z = n_col // CORES
    row, col = lax.axis_index("row"), lax.axis_index("col")
    row_steps = [1 << b for b in range(n_row.bit_length() - 1)]
    z_steps = [1 << b for b in range(n_z.bit_length() - 1)]

    def along_row(x, k):
        return lax.ppermute(x, "row", [(i, i ^ k) for i in range(n_row)])

    def along_z(x, k):
        return lax.ppermute(x, "col", [(i, i ^ (CORES * k)) for i in range(n_col)])

    def to_partner(x):
        return lax.ppermute(x, "col", [(i, i ^ 1) for i in range(n_col)])

    payload = pack(teacher, block_map, block_counts, interp_weights)
    student, unit, inverse = project(student_hidden, projection)
    rows = payload.shape[0]
    planes = [payload] + [along_z(payload, k) for k in range(1, n_z)]
    columns = doubled([student], along_row, row_steps[::-1])
    students = doubled([student], along_z, z_steps)
    partner_students = [to_partner(x) for x in students]
    offsets = [0]
    for step in row_steps[::-1]:
        offsets += [j ^ step for j in offsets]
    dests = jnp.stack(
        [row * n_col + (col ^ (CORES * k)) for k in range(n_z)]
        + [(row ^ j) * n_col + col for j in offsets[1:]]
    ).astype(jnp.int32)
    total = None
    early, late = [], []
    batches = []
    for k in range(n_z):
        order = row_steps[::-1] if k in REVERSED else row_steps
        held = doubled([planes[k]], along_row, order)
        halves = [(x, to_partner(x)) for x in held]
        if k < n_z - 2:
            batches.append([*halves[0], *halves[1]])
        else:
            early += halves[0]
            late += halves[1]
    batches = batches[:-1] + [sum(batches[-1:], []) + early]
    batches.append(late)
    for i, senders in enumerate(batches):
        n_last = n_z * tokens if i == len(batches) - 1 else None
        total = add_targets(total, senders, dests, tubes, per_peer, tokens, rows, n_last)
    own, column = total
    partner = to_partner(own)
    half = n_row // 2
    near = ((own, 0, tokens), (column, 0, (half - 1) * tokens))
    far = ((column, (half - 1) * tokens, half * tokens),)
    near_kinds = (F32,) + (BF16,) * (half - 1)
    far_kinds = (BF16,) * half
    sides = ((columns[0], near, near_kinds), (columns[1], far, far_kinds))
    sums = [
        relate(tokens, students, c, own, t, None, kinds)
        for c, t, kinds in sides
    ]
    blocks = []
    for i, (c, t, kinds) in enumerate(sides):
        blocks += relate(tokens, partner_students, c, partner, t, sums[i], kinds)
    arrived = [along_row(x, j) for j, x in zip(offsets[1:], blocks[1:])]
    turned = turn(projection)
    return finish(unit, inverse, turned, blocks[0], arrived)


def solution(mesh):
    in_specs = (
        P(("row", "col"), None),
        P(),
        P(("row", "col"), None),
        P(("row", "col"), None, None),
        P(("row", "col"), None),
        P(),
    )
    out_specs = P(("row", "col"), None)
    body = functools.partial(local, mesh.shape["row"], mesh.shape["col"])
    return jax.shard_map(body, mesh=mesh, in_specs=in_specs, out_specs=out_specs, check_vma=False)
```
